512 devices in a mesh: ctx: 64 (over z, x_hi, core), head: 8 (over y, x_lo).
Axes of the slice: x: 4 (x_hi: 2, x_lo: 2; x = x_hi * 2 + x_lo), y: 4, z: 16, core: 2. Of those that a mesh axis runs over, the one named last changes fastest.
Arguments:
- queries: bfloat16 [16384, 4096], P('ctx', 'head'), may hold values from -6 to 6
- keys: bfloat16 [16384, 1024], P('ctx', 'head'), may hold values from -6 to 6
- values: bfloat16 [16384, 1024], P('ctx', 'head'), may hold values from -36 to 36
- cotangent: bfloat16 [16384, 4096], P('ctx', 'head'), may hold values from -6 to 6
- gain: float32 [4096], P('head'), may hold values from 0.1 to 1.9
- key_blocks: int32 [128, 20], replicated, may hold values from -1 to 126, as said below
- span_order: int32 [128], replicated, may hold values from 0 to 127, as said below
Outputs:
- output: bfloat16 [16384, 4096], P('ctx', 'head')
- query_grad: bfloat16 [16384, 4096], P('ctx', 'head')
- key_grad: bfloat16 [16384, 1024], P('ctx', 'head')
- value_grad: bfloat16 [16384, 1024], P('ctx', 'head')
The draws below stay inside these ranges and needn't reach their ends.
Inputs may be any that keep to these rules, and one draw needn't show every extreme that they name: `span_order`: a permutation of the storage blocks' sequence blocks. `key_blocks`: row b names distinct sequence blocks, each less than b, and -1 in empty slots, which come last in a row. Over the rows of the sequence blocks held by the 2 storage blocks of one device, the named blocks never include two different blocks that lie on one same device.
All inputs are finite; a program needn't handle non-finite values.
Results may differ from the reference program's by a relative error of at most 0.0058.
Values may be sent and summed in bfloat16 or wider, within the bound.
No kernel may reach another device: no remote copies, remote signals or barrier semaphores. Data moves between devices by JAX's collectives and lax.ppermute only.
A program may use at most 64 MiB of HBM per device.

```python
import math
import jax
import jax.numpy as jnp
from jax import lax

DH = 128
GROUP = 4
BLOCK = 128
TOK_DEV = 256
FAR = 20
KVH = 8
QH = 32
TOKENS = 16384
NB = 128


def shared_order(key):
    return jax.random.permutation(jax.random.fold_in(key, 11), NB).astype(jnp.int32)


def draw_span_order(key, part):
    return shared_order(key)


def draw_key_blocks(key, part):
    per_device = TOK_DEV // BLOCK
    device_count = NB // per_device
    seq_order = shared_order(key)
    placement = jnp.argsort(seq_order).astype(jnp.int32)
    picked = jax.random.randint(jax.random.fold_in(key, 12), (device_count, device_count), 0, per_device).astype(jnp.int32)
    first_home = placement[0] // per_device
    late_home = placement[NB - 2] // per_device
    device_ids = jnp.arange(device_count, dtype=jnp.int32)
    picked = jnp.where(device_ids[None, :] == first_home, placement[0] % per_device, picked)
    picked = jnp.where(device_ids[None, :] == late_home, placement[NB - 2] % per_device, picked)
    candidate = seq_order[device_ids[None, :] * per_device + picked]
    holder = placement // per_device
    row_candidates = candidate[holder]
    sequence = jnp.arange(NB, dtype=jnp.int32)[:, None]
    usable = row_candidates < sequence
    noise_rank = jax.random.randint(jax.random.fold_in(key, 13), (NB, device_count), 1, 4096).astype(jnp.int32)
    favoured = (row_candidates == 0) | (row_candidates == NB - 2)
    ranking = jnp.where(favoured, 0, noise_rank) * device_count + device_ids[None, :]
    ranking = jnp.where(usable, ranking, 4096 * device_count + device_ids[None, :])
    chosen_at = jnp.argsort(ranking, axis=1)[:, :FAR]
    chosen = jnp.take_along_axis(row_candidates, chosen_at, axis=1)
    kept_slot = jnp.take_along_axis(usable, chosen_at, axis=1)
    return jnp.where(kept_slot, chosen, -1).astype(jnp.int32)


def draw_values(key, part):
    columns = KVH * DH
    head_of = (jnp.arange(columns) // DH).astype(jnp.float32)
    rising = 3.0 ** (head_of / max(KVH - 1, 1))
    spread = jnp.exp(jax.random.uniform(jax.random.fold_in(key, 21), (columns,), minval=0.0, maxval=math.log(10.0)))
    noise_field = jnp.clip(jax.random.normal(jax.random.fold_in(key, 22), (TOKENS, columns)), -4.0, 4.0)
    return (0.3 * noise_field * rising * spread).astype(jnp.bfloat16)


def steps_of(stream_key, dims, cuts, least, high):
    def one(position, shards_of):
        steps = jax.random.uniform(jax.random.fold_in(jax.random.fold_in(stream_key, 6), position), (shards_of,), jnp.float32, least / len(cuts), high / len(cuts))
        return jnp.repeat(jnp.exp(steps), dims[position] // shards_of).reshape((-1,) + (1,) * (len(dims) - position - 1))

    level = one(*cuts[0])
    for cut in cuts[1:]:
        level = level * one(*cut)
    return level


def centred(stream_key, extent, scale, reach, split=(), kind=jnp.bfloat16):
    level = steps_of(stream_key, extent, split, -0.22, 0.18) if split else 1.0
    array = jax.random.normal(stream_key, extent, jnp.float32) * scale * level
    return jnp.minimum(jnp.maximum(array, -reach), reach).astype(kind)


def setup_inputs(seed: int = 0) -> dict:
    arg_keys = jax.random.split(jax.random.key(seed), 8)
    return {
        "queries": centred(arg_keys[0], (TOKENS, QH * DH), 1.0, 6.0, ((0, 64), (1, 8))),
        "keys": centred(arg_keys[1], (TOKENS, KVH * DH), 1.0, 6.0, ((0, 64), (1, 8))),
        "values": draw_values(jax.random.fold_in(arg_keys[7], 71), 0),
        "cotangent": centred(arg_keys[3], (TOKENS, QH * DH), 1.0, 6.0, ((0, 64), (1, 8))),
        "gain": jnp.clip(1.0 + 0.18 * jax.random.normal(arg_keys[4], (QH * DH,), jnp.float32), 0.1, 1.9),
        "key_blocks": draw_key_blocks(jax.random.fold_in(arg_keys[7], 71), 0),
        "span_order": draw_span_order(jax.random.fold_in(arg_keys[7], 71), 0),
    }


def pair_weights(query_block, key_sel, allowed, score_scale, score_shift):
    scores = jnp.einsum('qhgd,skhd->shgqk', query_block.astype(jnp.float32), key_sel.astype(jnp.float32))
    return jnp.where(allowed[:, None, None], jax.nn.sigmoid(scores * score_scale - score_shift), 0.0)

def reference(queries, keys, values, cotangent, gain, key_blocks, span_order):
    key_heads = keys.shape[1] // DH
    query_blocks = queries.reshape(NB, BLOCK, key_heads, GROUP, DH)
    key_store = keys.reshape(NB, BLOCK, key_heads, DH)
    value_store = values.reshape(NB, BLOCK, key_heads, DH)
    placement = jnp.argsort(span_order).astype(jnp.int32)
    far_seq = key_blocks[span_order]
    far_live = far_seq >= 0
    far_store = placement[jnp.maximum(far_seq, 0)].astype(jnp.int32)
    slot_store = jnp.concatenate([jnp.arange(NB, dtype=jnp.int32)[:, None], far_store], axis=1)
    slot_live = jnp.concatenate([jnp.ones((NB, 1), dtype=bool), far_live], axis=1)
    positions = jnp.arange(BLOCK, dtype=jnp.int32)
    causal = positions[None, :] <= positions[:, None]
    first_slot = (jnp.arange(FAR + 1, dtype=jnp.int32) == 0)[:, None, None]
    score_scale = 1.0 / math.sqrt(DH)
    score_shift = math.log(BLOCK * (FAR + 1))

    def allowed_of(live_row):
        return jnp.where(first_slot, causal[None], live_row[:, None, None])

    def forward_block(inputs):
        query_block, store_row, live_row = inputs
        weight = pair_weights(query_block, key_store[store_row], allowed_of(live_row), score_scale, score_shift)
        weight_low = weight.astype(jnp.bfloat16)
        return jnp.einsum('shgqk,skhd->qhgd', weight_low.astype(jnp.float32), value_store[store_row].astype(jnp.float32))
    attended = lax.map(forward_block, (query_blocks, slot_store, slot_live)).reshape(TOKENS, QH * DH)
    inverse_rms = lax.rsqrt(lax.optimization_barrier(jnp.mean(attended * attended, axis=1, keepdims=True)) + 1e-06)
    output = (attended * inverse_rms * gain).astype(jnp.bfloat16)
    grad_in = cotangent.astype(jnp.float32) * gain
    inner_mean = lax.optimization_barrier(jnp.mean(grad_in * attended, axis=1, keepdims=True))
    grad_att = (inverse_rms * (grad_in - attended * inverse_rms * inverse_rms * inner_mean)).astype(jnp.bfloat16)
    grad_blocks = grad_att.reshape(NB, BLOCK, key_heads, GROUP, DH)

    def backward_block(state_carry, inputs):
        key_acc, value_acc = state_carry
        query_block, grad_block, store_row, live_row = inputs
        key_sel = key_store[store_row]
        value_sel = value_store[store_row]
        weight = pair_weights(query_block, key_sel, allowed_of(live_row), score_scale, score_shift)
        weight_low = weight.astype(jnp.bfloat16)
        grad_weight = jnp.einsum('qhgd,skhd->shgqk', grad_block.astype(jnp.float32), value_sel.astype(jnp.float32))
        grad_score = (grad_weight * weight * (1.0 - weight)).astype(jnp.bfloat16)
        query_part = jnp.einsum('shgqk,skhd->qhgd', grad_score.astype(jnp.float32), key_sel.astype(jnp.float32)) * score_scale
        key_part = jnp.einsum('shgqk,qhgd->skhd', grad_score.astype(jnp.float32), query_block.astype(jnp.float32)) * score_scale
        value_part = jnp.einsum('shgqk,qhgd->skhd', weight_low.astype(jnp.float32), grad_block.astype(jnp.float32))
        key_acc = key_acc.at[store_row].add(key_part)
        value_acc = value_acc.at[store_row].add(value_part)
        return ((key_acc, value_acc), query_part.astype(jnp.bfloat16))
    zero_acc = jnp.zeros((NB, BLOCK, key_heads, DH), jnp.float32)
    (key_acc, value_acc), query_grad = lax.scan(backward_block, (zero_acc, zero_acc), (query_blocks, grad_blocks, slot_store, slot_live))
    return (output, query_grad.reshape(TOKENS, QH * DH), key_acc.reshape(TOKENS, KVH * DH).astype(jnp.bfloat16), value_acc.reshape(TOKENS, KVH * DH).astype(jnp.bfloat16))
```

```python
import math

import jax
import jax.numpy as jnp
from jax import lax
from jax.experimental import pallas as pl
from jax.experimental.pallas import tpu as pltpu
from jax.sharding import Mesh, PartitionSpec as P

DH = 128
BLOCK = 128
CTX = ("z", "xh", "core")
HEAD = ("y", "xl")
RING = ("z", "core")
NZ = 16
HALF = NZ // 2
SWAP = [(0, 1), (1, 0)]
NBLK = 128
DUMP = NBLK
PART = 4 * BLOCK
PARTS = 32
SWAP_AFTER = (4, 7)
GATHERED = [1] * 16 + [8, 6, 1, 1]
SENT = [16, 10, 4, 1, 1]
F32 = jnp.float32
BF16 = jnp.bfloat16


def ring_pairs():
    return [
        (z * 2 + c, ((z + (1 if c == 0 else -1)) % NZ) * 2 + c) for z in range(NZ) for c in range(2)
    ]


def ring(x):
    return lax.ppermute(x, RING, ring_pairs())


def swap(x):
    return lax.ppermute(x, "core", SWAP)


def gather_blocks(kv):
    pair = jnp.concatenate([kv, lax.ppermute(kv, "xh", SWAP)], axis=0)
    own, other = pair, swap(pair)
    chunk, mine, theirs = [own, other], [], []
    waiting = []
    for s in range(1, HALF):
        own, other = ring(own), ring(other)
        mine += [own, other]
        waiting += [other, own]
        if s in SWAP_AFTER:
            theirs.append(swap(jnp.concatenate(waiting, axis=0)))
            waiting = []
    far = ring(own)
    return chunk + mine + theirs + [far, swap(far)]


def total(*terms):
    out = terms[0].astype(F32)
    for t in terms[1:]:
        out = out + t.astype(F32)
    return out


def part_of(array, i):
    return array[i * PART : (i + 1) * PART]


def scatter_blocks(mine, near, middle, far, far_theirs):
    own, other = total(far, swap(far_theirs)).astype(BF16), None
    middle, near = swap(middle), swap(near)
    for s in range(HALF - 2, -1, -1):
        theirs, i = (middle, 2 * s - 10) if s > 4 else (near, 2 * s)
        own = total(ring(own), part_of(mine, 2 + 2 * s), part_of(theirs, i + 1)).astype(BF16)
        own, later_mine, later_theirs = lax.optimization_barrier((own, mine, theirs))
        first = [] if other is None else [ring(other)]
        other = total(*first, part_of(later_mine, 3 + 2 * s), part_of(later_theirs, i)).astype(BF16)
    other = total(ring(other), part_of(mine, 1)).astype(BF16)
    keep = total(ring(own), part_of(mine, 0), swap(other))
    rows = PART // 2
    mate = lax.ppermute(keep[rows:].astype(BF16), "xh", SWAP)
    return keep[:rows] + mate.astype(F32)


def head_sum(x):
    return lax.psum(x, HEAD)


def positions(key_blocks, span_order, per_device):
    z, xh, core = (lax.axis_index(n) for n in CTX)
    me = (z * 2 + xh) * 2 + core
    seq = lax.dynamic_slice(span_order, (me * per_device,), (per_device,))
    pick = (seq[:, None] == jnp.arange(NBLK)[None, :]).astype(jnp.int32)
    far = jnp.sum(pick[:, :, None] * key_blocks[None], axis=1)
    where = jnp.arange(NBLK, dtype=jnp.int32)
    store = jnp.sum(
        jnp.where(far[:, :, None] == span_order[None, None, :], where[None, None, :], 0), axis=2
    )
    own = me * per_device + jnp.arange(per_device, dtype=jnp.int32)
    store = jnp.concatenate([own[:, None], store], axis=1)
    live = jnp.concatenate([jnp.ones((per_device, 1), bool), far >= 0], axis=1)
    owner, half = store // per_device, store % per_device
    oz, oxh, ocore = owner // 4, (owner // 2) % 2, owner % 2
    dz = (oz - z + HALF) % NZ - HALF
    inner = (oxh ^ xh) * 2 + half
    dist = jnp.abs(dz)

    across = ocore ^ core

    def locate(first_group):
        chunk = jnp.where(first_group, 0, 14) + 2 * dist
        chunk = jnp.where(dist == 0, 0, jnp.where(dist == HALF, 30, chunk))
        return jnp.where(live, (chunk + across) * 4 + inner, DUMP).astype(jnp.int32)

    return locate((dz < 0) == (core == 0)), locate((dz > 0) == (core == 0))


def rows_of(spot):
    return pl.ds(pl.multiple_of(spot * BLOCK, BLOCK), BLOCK)


def contract_first(a, b):
    return lax.dot_general(a, b, (((0,), (0,)), ((), ())), preferred_element_type=F32)


def dot(a, b):
    return jnp.dot(a, b, preferred_element_type=F32)


def heads_of(ref, q, n):
    return [ref[pl.ds(q * BLOCK, BLOCK), h * DH : (h + 1) * DH] for h in range(n)]


def spans(counts):
    ends = [sum(counts[: i + 1]) for i in range(len(counts))]
    return [pl.ds((e - n) * PART, n * PART) for e, n in zip(ends, counts)]


def load_set(sources, held, sems):
    copies = [
        pltpu.make_async_copy(s, held.at[span, :], sems.at[i])
        for i, (s, span) in enumerate(zip(sources, spans(GATHERED)))
    ]
    for c in copies:
        c.start()
    held[DUMP * BLOCK :, :] = jnp.zeros((BLOCK, 2 * DH), BF16)
    return copies


def steps_at(i):
    if isinstance(i, int) and i == 0:
        return 0, BLOCK
    return pl.multiple_of(BLOCK + 2 * BLOCK * (i - 1), BLOCK), 2 * BLOCK


def causal_mask(width):
    key = lax.broadcasted_iota(jnp.int32, (BLOCK, width), 0)
    row = lax.broadcasted_iota(jnp.int32, (BLOCK, width), 1) % BLOCK
    return key <= row


def forward_kernel(pairs, scale, shift, pos, queries, cotangent, gain, *rest):
    n = len(GATHERED)
    sources, (attended, stored, sums), scratch = rest[:n], rest[n : n + 3], rest[n + 3 :]
    held, weights, sems, out_sems = scratch
    per_device, slots = pos.shape
    group = queries.shape[1] // DH
    width = group * BLOCK
    copies = load_set(sources, held, sems)
    query_t = [
        jnp.concatenate([x.T for x in heads_of(queries, q, group)], axis=1)
        for q in range(per_device)
    ]
    for c in copies:
        c.wait()

    def weigh(keys, query):
        score = dot(keys, query)
        return 1.0 / (1.0 + jnp.exp(shift - score * scale))

    def save(q, i):
        span = pl.ds(*steps_at(i))
        return pltpu.make_async_copy(
            weights.at[q, span, :], stored.at[q, span, :], out_sems.at[q, i]
        )

    for q in range(per_device):
        own = held[rows_of(pos[q, 0]), :]
        weight = jnp.where(causal_mask(width), weigh(own[:, :DH], query_t[q]), 0.0)
        weights[q, :BLOCK, :] = weight
        save(q, 0).start()
        attended[q] = contract_first(own[:, DH:], weight.astype(BF16))

        def step(i, carry):
            two = jnp.concatenate(
                [held[rows_of(pos[q, 1 + 2 * i]), :], held[rows_of(pos[q, 2 + 2 * i]), :]], axis=0
            )
            weight = weigh(two[:, :DH], query_t[q])
            weights[q, pl.ds(*steps_at(i + 1)), :] = weight
            save(q, i + 1).start()
            attended[q] += contract_first(two[:, DH:], weight.astype(BF16))
            return carry

        lax.fori_loop(0, pairs, step, 0, unroll=2)
        att = attended[q]
        grad_in = jnp.concatenate(
            [
                (x.astype(F32) * gain[:, h * DH : (h + 1) * DH]).T
                for h, x in enumerate(heads_of(cotangent, q, group))
            ],
            axis=1,
        )
        for i, value in enumerate((att * att, grad_in * att)):
            col = jnp.sum(value, axis=0, keepdims=True)
            row = col[:, :BLOCK]
            for h in range(1, group):
                row = row + col[:, h * BLOCK : (h + 1) * BLOCK]
            sums[2 * q + i : 2 * q + i + 1, :] = row
    for q in range(per_device):
        for i in range(pairs + 1):
            save(q, i).wait()


def backward_kernel(
    pairs, scale, columns, kpos, gpos, sums, queries, cotangent, gain, attended, stored, *rest
):
    n, m = len(GATHERED), len(SENT)
    sources, rest = rest[:n], rest[n:]
    output, query_grad = rest[:2]
    parts = rest[2 : m + 2]
    held, acc, stage, weights, sems, out_sems, weight_sems = rest[m + 2 :]
    per_device = kpos.shape[0]
    group = queries.shape[1] // DH
    copies = load_set(sources, held, sems)

    def fetch(q, i):
        span = pl.ds(*steps_at(i))
        return pltpu.make_async_copy(
            stored.at[q, span, :], weights.at[q, span, :], weight_sems.at[q, i]
        )

    for q in range(per_device):
        for i in range(pairs + 1):
            fetch(q, i).start()
    acc[...] = jnp.zeros(acc.shape, F32)
    grads_t, grads, stacked = [], [], []
    for q in range(per_device):
        inverse = lax.rsqrt(sums[2 * q : 2 * q + 1, :] / columns + 1e-6)
        inner = sums[2 * q + 1 : 2 * q + 2, :] / columns
        back = inverse * inverse * inner
        grad_t, grad = [], []
        for h, x in enumerate(heads_of(cotangent, q, group)):
            gain_h = gain[:, h * DH : (h + 1) * DH]
            att = attended[q, :, h * BLOCK : (h + 1) * BLOCK]
            grad_in = (x.astype(F32) * gain_h).T
            low = inverse * (grad_in - att * back)
            grad_t.append(low.astype(BF16))
            grad.append(low.T.astype(BF16))
            output[pl.ds(q * BLOCK, BLOCK), h * DH : (h + 1) * DH] = (
                (att * inverse).T * gain_h
            ).astype(BF16)
        grads_t.append(jnp.concatenate(grad_t, axis=1))
        grads.append(jnp.concatenate(grad, axis=0))
        stacked.append(jnp.concatenate(heads_of(queries, q, group), axis=0))
    for c in copies:
        c.wait()

    def pair_grads(q, both, weight):
        low = weight.astype(BF16)
        grad_weight = dot(both[:, DH:], grads_t[q])
        grad_score = (grad_weight * (weight * (1.0 - weight))).astype(BF16)
        part = jnp.concatenate([dot(grad_score, stacked[q]) * scale, dot(low, grads[q])], axis=1)
        return contract_first(both[:, :DH], grad_score), part

    for q in range(per_device):
        own = held[rows_of(kpos[q, 0]), :]
        fetch(q, 0).wait()
        query_part, part = pair_grads(q, own, weights[q, :BLOCK, :])
        acc[rows_of(gpos[q, 0]), :] += part

        def step(i, query_part):
            two = jnp.concatenate(
                [held[rows_of(kpos[q, 1 + 2 * i]), :], held[rows_of(kpos[q, 2 + 2 * i]), :]], axis=0
            )
            fetch(q, i + 1).wait()
            more, part = pair_grads(q, two, weights[q, pl.ds(*steps_at(i + 1)), :])
            acc[rows_of(gpos[q, 1 + 2 * i]), :] += part[:BLOCK]
            acc[rows_of(gpos[q, 2 + 2 * i]), :] += part[BLOCK:]
            return query_part + more

        query_part = lax.fori_loop(0, pairs, step, query_part, unroll=2)
        for h in range(group):
            query_grad[pl.ds(q * BLOCK, BLOCK), h * DH : (h + 1) * DH] = (
                query_part[:, h * BLOCK : (h + 1) * BLOCK].T * scale
            ).astype(BF16)

    outs = []
    for i in (4, 3, 2, 1, 0):
        span = spans(SENT)[i]
        stage[span, :] = acc[span, :].astype(BF16)
        copy = pltpu.make_async_copy(stage.at[span, :], parts[i], out_sems.at[i])
        copy.start()
        outs.append(copy)
    for c in outs:
        c.wait()


def body(queries, keys, values, cotangent, gain, key_blocks, span_order):
    row_count, query_width = queries.shape
    key_width = keys.shape[1]
    group = query_width // key_width
    per_device = row_count // BLOCK
    slots = key_blocks.shape[1] + 1
    pairs = (slots - 1) // 2
    scale = 1.0 / math.sqrt(DH)
    shift = math.log(BLOCK * slots)
    gain = gain.reshape(1, query_width)

    gathered = gather_blocks(jnp.concatenate([keys, values], axis=1))
    kpos, gpos = positions(key_blocks, span_order, per_device)

    smem = pl.BlockSpec(memory_space=pltpu.SMEM)
    vmem = pl.BlockSpec(memory_space=pltpu.VMEM)
    anyw = pl.BlockSpec(memory_space=pl.ANY)
    wide = group * BLOCK
    set_scratch = [
        pltpu.VMEM(((NBLK + 1) * BLOCK, 2 * DH), BF16),
    ]
    flops = 2 * slots * per_device * wide * BLOCK * DH

    attended, weights, sums = pl.pallas_call(
        lambda *refs: forward_kernel(pairs, scale, shift, *refs),
        out_shape=(
            jax.ShapeDtypeStruct((per_device, DH, wide), F32),
            jax.ShapeDtypeStruct((per_device, slots * BLOCK, wide), F32),
            jax.ShapeDtypeStruct((2 * per_device, BLOCK), F32),
        ),
        in_specs=[smem, vmem, vmem, vmem] + [anyw] * len(GATHERED),
        out_specs=(vmem, anyw, vmem),
        scratch_shapes=set_scratch
        + [
            pltpu.VMEM((per_device, slots * BLOCK, wide), F32),
            pltpu.SemaphoreType.DMA((len(GATHERED),)),
            pltpu.SemaphoreType.DMA((per_device, pairs + 1)),
        ],
        compiler_params=pltpu.CompilerParams(vmem_limit_bytes=40 << 20),
        cost_estimate=pl.CostEstimate(flops=2 * flops, bytes_accessed=16 << 20, transcendentals=0),
        name="forward",
    )(kpos, queries, cotangent, gain, *gathered)

    sums = head_sum(sums)

    results = pl.pallas_call(
        lambda *refs: backward_kernel(
            pairs, scale, float(query_width * lax.axis_size(HEAD)), *refs
        ),
        out_shape=(
            jax.ShapeDtypeStruct((row_count, query_width), BF16),
            jax.ShapeDtypeStruct((row_count, query_width), BF16),
            *[jax.ShapeDtypeStruct((n * PART, 2 * DH), BF16) for n in SENT],
        ),
        in_specs=[smem, smem] + [vmem] * 5 + [anyw] + [anyw] * len(GATHERED),
        out_specs=(vmem, vmem) + (anyw,) * len(SENT),
        scratch_shapes=set_scratch
        + [
            pltpu.VMEM(((NBLK + 1) * BLOCK, 2 * DH), F32),
            pltpu.VMEM((NBLK * BLOCK, 2 * DH), BF16),
            pltpu.VMEM((per_device, slots * BLOCK, wide), F32),
            pltpu.SemaphoreType.DMA((len(GATHERED),)),
            pltpu.SemaphoreType.DMA((len(SENT),)),
            pltpu.SemaphoreType.DMA((per_device, pairs + 1)),
        ],
        compiler_params=pltpu.CompilerParams(vmem_limit_bytes=56 << 20),
        cost_estimate=pl.CostEstimate(flops=5 * flops, bytes_accessed=32 << 20, transcendentals=0),
        name="backward",
    )(kpos, gpos, sums, queries, cotangent, gain, attended, weights, *gathered)
    output, query_grad, parts = results[0], results[1], results[2:]
    grads = scatter_blocks(*parts).astype(BF16)
    return output, query_grad, grads[:, :key_width], grads[:, key_width:]


def solution(mesh):
    fine = Mesh(mesh.devices.reshape(NZ, 2, 2, 4, 2), CTX + HEAD)
    tok = P(CTX, HEAD)
    return jax.shard_map(
        body,
        mesh=fine,
        in_specs=(tok, tok, tok, tok, P(HEAD), P(), P()),
        out_specs=(tok, tok, tok, tok),
        check_vma=False,
    )
```

```python
import math

import jax
import jax.numpy as jnp
from jax import lax
from jax.experimental import pallas as pl
from jax.experimental.pallas import tpu as pltpu
from jax.sharding import Mesh, PartitionSpec as P

DH = 128
BLOCK = 128
CTX = ("z", "xh", "core")
HEAD = ("y", "xl")
RING = ("z", "core")
NZ = 16
HALF = NZ // 2
SWAP = [(0, 1), (1, 0)]
NBLK = 128
PART = 4 * BLOCK
PARTS = 32
SWAP_AFTER = (4, 7)
GATHERED = [1] * 16 + [8, 6, 1, 1]
SENT = [16, 10, 4, 1, 1]
F32 = jnp.float32
BF16 = jnp.bfloat16


def ring_pairs():
    return [
        (z * 2 + c, ((z + (1 if c == 0 else -1)) % NZ) * 2 + c) for z in range(NZ) for c in range(2)
    ]


def ring(x):
    return lax.ppermute(x, RING, ring_pairs())


def swap(x):
    return lax.ppermute(x, "core", SWAP)


def gather_blocks(kv):
    pair = jnp.concatenate([kv, lax.ppermute(kv, "xh", SWAP)], axis=0)
    own, other = pair, swap(pair)
    chunk, mine, theirs = [own, other], [], []
    waiting = []
    for s in range(1, HALF):
        own, other = ring(own), ring(other)
        mine += [own, other]
        waiting += [other, own]
        if s in SWAP_AFTER:
            theirs.append(swap(jnp.concatenate(waiting, axis=0)))
            waiting = []
    far = ring(own)
    return chunk + mine + theirs + [far, swap(far)]


def total(*terms):
    out = terms[0].astype(F32)
    for t in terms[1:]:
        out = out + t.astype(F32)
    return out


def part_of(array, i):
    return array[i * PART : (i + 1) * PART]


def scatter_blocks(mine, near, middle, far, far_theirs):
    own, other = total(far, swap(far_theirs)).astype(BF16), None
    middle, near = swap(middle), swap(near)
    for s in range(HALF - 2, -1, -1):
        theirs, i = (middle, 2 * s - 10) if s > 4 else (near, 2 * s)
        own = total(ring(own), part_of(mine, 2 + 2 * s), part_of(theirs, i + 1)).astype(BF16)
        own, later_mine, later_theirs = lax.optimization_barrier((own, mine, theirs))
        first = [] if other is None else [ring(other)]
        other = total(*first, part_of(later_mine, 3 + 2 * s), part_of(later_theirs, i)).astype(BF16)
    other = total(ring(other), part_of(mine, 1)).astype(BF16)
    keep = total(ring(own), part_of(mine, 0), swap(other))
    rows = PART // 2
    mate = lax.ppermute(keep[rows:].astype(BF16), "xh", SWAP)
    return keep[:rows] + mate.astype(F32)


def head_copies(x):
    return lax.all_to_all(x, HEAD, 0, 0, tiled=True)


def positions(key_blocks, span_order, per_device):
    z, xh, core = (lax.axis_index(n) for n in CTX)
    me = (z * 2 + xh) * 2 + core
    seq = lax.dynamic_slice(span_order, (me * per_device,), (per_device,))
    pick = (seq[:, None] == jnp.arange(NBLK)[None, :]).astype(jnp.int32)
    far = jnp.sum(pick[:, :, None] * key_blocks[None], axis=1)
    where = jnp.arange(NBLK, dtype=jnp.int32)
    store = jnp.sum(
        jnp.where(far[:, :, None] == span_order[None, None, :], where[None, None, :], 0), axis=2
    )
    own = me * per_device + jnp.arange(per_device, dtype=jnp.int32)
    store = jnp.concatenate([own[:, None], store], axis=1)
    live = jnp.concatenate([jnp.ones((per_device, 1), bool), far >= 0], axis=1)
    owner, half = store // per_device, store % per_device
    oz, oxh, ocore = owner // 4, (owner // 2) % 2, owner % 2
    dz = (oz - z + HALF) % NZ - HALF
    inner = (oxh ^ xh) * 2 + half
    dist = jnp.abs(dz)

    across = ocore ^ core

    def locate(first_group):
        chunk = jnp.where(first_group, 0, 14) + 2 * dist
        chunk = jnp.where(dist == 0, 0, jnp.where(dist == HALF, 30, chunk))
        return jnp.where(live, (chunk + across) * 4 + inner, NBLK).reshape(-1)

    def holder(spot):
        match = spot[None, :] == jnp.arange(NBLK, dtype=jnp.int32)[:, None]
        return jnp.max(jnp.where(match, slot[None, :], -1), axis=1)

    source = locate((dz < 0) == (core == 0))
    count = source.shape[0]
    order = jnp.arange(count, dtype=jnp.int32)
    same = source[:, None] == source[None, :]
    first = jnp.min(jnp.where(same, order[None, :], count), axis=1)
    slot = jnp.where(source == NBLK, count, first).astype(jnp.int32)
    back = locate((dz > 0) == (core == 0))
    return slot.reshape(per_device, -1), holder(source), holder(back)


def rows_of(spot):
    return pl.ds(pl.multiple_of(spot * BLOCK, BLOCK), BLOCK)


def contract_first(a, b):
    return lax.dot_general(a, b, (((0,), (0,)), ((), ())), preferred_element_type=F32)


def dot(a, b):
    return jnp.dot(a, b, preferred_element_type=F32)


def heads_of(ref, q, n):
    return [ref[pl.ds(q * BLOCK, BLOCK), h * DH : (h + 1) * DH] for h in range(n)]


def each_block(counts, visit):
    base = 0
    for k, n in enumerate(counts):

        def one(i, carry, k=k, base=base):
            visit(k, i, base + i)
            return carry

        lax.fori_loop(0, 4 * n, one, 0)
        base += 4 * n


def steps_at(i):
    if isinstance(i, int) and i == 0:
        return 0, BLOCK
    return pl.multiple_of(BLOCK + 2 * BLOCK * (i - 1), BLOCK), 2 * BLOCK


def causal_mask(width):
    key = lax.broadcasted_iota(jnp.int32, (BLOCK, width), 0)
    row = lax.broadcasted_iota(jnp.int32, (BLOCK, width), 1) % BLOCK
    return key <= row


def forward_kernel(pairs, scale, shift, slots, holder, queries, cotangent, gain, *rest):
    n = len(GATHERED)
    sources, (attended, weights, held, sums, sems) = rest[:n], rest[n:]
    per_device = slots.shape[0]
    spare = per_device * slots.shape[1]
    group = queries.shape[1] // DH
    width = group * BLOCK

    def fetch(k, i, at):
        @pl.when(holder[at] >= 0)
        def _():
            pltpu.make_async_copy(
                sources[k].at[rows_of(i), :], held.at[rows_of(holder[at]), :], sems.at[holder[at]]
            ).start()

    def await_slot(q, j):
        mine = slots[q, j]

        @pl.when(mine == q * slots.shape[1] + j)
        def _():
            pltpu.make_async_copy(
                sources[0].at[:BLOCK, :], held.at[rows_of(mine), :], sems.at[mine]
            ).wait()

        return held[rows_of(mine), :]

    each_block(GATHERED, fetch)
    held[spare * BLOCK :, :] = jnp.zeros((BLOCK, 2 * DH), BF16)
    query_t = [
        jnp.concatenate([x.T for x in heads_of(queries, q, group)], axis=1)
        for q in range(per_device)
    ]

    def weigh(keys, query):
        score = dot(keys, query)
        return 1.0 / (1.0 + jnp.exp(shift - score * scale))

    for q in range(per_device):
        own = await_slot(q, 0)
        weight = jnp.where(causal_mask(width), weigh(own[:, :DH], query_t[q]), 0.0)
        weights[q, :BLOCK, :] = weight
        attended[q] = contract_first(own[:, DH:], weight.astype(BF16))

        def step(i, carry):
            two = jnp.concatenate([await_slot(q, 1 + 2 * i), await_slot(q, 2 + 2 * i)], axis=0)
            weight = weigh(two[:, :DH], query_t[q])
            weights[q, pl.ds(*steps_at(i + 1)), :] = weight
            attended[q] += contract_first(two[:, DH:], weight.astype(BF16))
            return carry

        lax.fori_loop(0, pairs, step, 0, unroll=True)
        att = attended[q]
        grad_in = jnp.concatenate(
            [
                (x.astype(F32) * gain[:, h * DH : (h + 1) * DH]).T
                for h, x in enumerate(heads_of(cotangent, q, group))
            ],
            axis=1,
        )
        for i, value in enumerate((att * att, grad_in * att)):
            col = jnp.sum(value, axis=0, keepdims=True)
            row = col[:, :BLOCK]
            for h in range(1, group):
                row = row + col[:, h * BLOCK : (h + 1) * BLOCK]
            sums[:, 2 * q + i : 2 * q + i + 1, :] = jnp.broadcast_to(
                row[None], (sums.shape[0], 1, BLOCK)
            )


def backward_kernel(
    pairs, scale, columns, slots, holder, sums, queries, cotangent, gain, attended, weights, held, *rest
):
    m = len(SENT)
    output, query_grad = rest[:2]
    parts = rest[2 : m + 2]
    acc, stage, zero, sems = rest[m + 2 :]
    per_device = slots.shape[0]
    group = queries.shape[1] // DH
    zero[...] = jnp.zeros(zero.shape, BF16)

    def clear(k, i, at):
        return pltpu.make_async_copy(zero, parts[k].at[rows_of(i), :], sems.at[0])

    def send(k, i, at):
        return pltpu.make_async_copy(
            stage.at[rows_of(holder[at]), :], parts[k].at[rows_of(i), :], sems.at[1]
        )

    def over_blocks(action, copy, held_ones):
        def visit(k, i, at):
            @pl.when((holder[at] >= 0) == held_ones)
            def _():
                getattr(copy(k, i, at), action)()

        each_block(SENT, visit)

    over_blocks("start", clear, False)
    acc[...] = jnp.zeros(acc.shape, F32)
    grads_t, grads, stacked = [], [], []
    for q in range(per_device):
        inverse = lax.rsqrt(jnp.sum(sums[:, 2 * q, :], axis=0, keepdims=True) / columns + 1e-6)
        inner = jnp.sum(sums[:, 2 * q + 1, :], axis=0, keepdims=True) / columns
        back = inverse * inverse * inner
        grad_t, grad = [], []
        for h, x in enumerate(heads_of(cotangent, q, group)):
            gain_h = gain[:, h * DH : (h + 1) * DH]
            att = attended[q, :, h * BLOCK : (h + 1) * BLOCK]
            grad_in = (x.astype(F32) * gain_h).T
            low = inverse * (grad_in - att * back)
            grad_t.append(low.astype(BF16))
            grad.append(low.T.astype(BF16))
            output[pl.ds(q * BLOCK, BLOCK), h * DH : (h + 1) * DH] = (
                (att * inverse).T * gain_h
            ).astype(BF16)
        grads_t.append(jnp.concatenate(grad_t, axis=1))
        grads.append(jnp.concatenate(grad, axis=0))
        stacked.append(jnp.concatenate(heads_of(queries, q, group), axis=0))
    def pair_grads(q, both, weight):
        low = weight.astype(BF16)
        grad_weight = dot(both[:, DH:], grads_t[q])
        grad_score = (grad_weight * (weight * (1.0 - weight))).astype(BF16)
        part = jnp.concatenate([dot(grad_score, stacked[q]) * scale, dot(low, grads[q])], axis=1)
        return contract_first(both[:, :DH], grad_score), part

    for q in range(per_device):
        own = held[rows_of(slots[q, 0]), :]
        query_part, part = pair_grads(q, own, weights[q, :BLOCK, :])
        acc[rows_of(slots[q, 0]), :] += part

        def step(i, query_part):
            two = jnp.concatenate(
                [held[rows_of(slots[q, 1 + 2 * i]), :], held[rows_of(slots[q, 2 + 2 * i]), :]], axis=0
            )
            more, part = pair_grads(q, two, weights[q, pl.ds(*steps_at(i + 1)), :])
            acc[rows_of(slots[q, 1 + 2 * i]), :] += part[:BLOCK]
            acc[rows_of(slots[q, 2 + 2 * i]), :] += part[BLOCK:]
            return query_part + more

        query_part = lax.fori_loop(0, pairs, step, query_part, unroll=True)
        for h in range(group):
            query_grad[pl.ds(q * BLOCK, BLOCK), h * DH : (h + 1) * DH] = (
                query_part[:, h * BLOCK : (h + 1) * BLOCK].T * scale
            ).astype(BF16)

    stage[...] = acc[: stage.shape[0], :].astype(BF16)
    over_blocks("start", send, True)
    over_blocks("wait", send, True)
    over_blocks("wait", clear, False)


def specs():
    return tuple(pl.BlockSpec(memory_space=m) for m in (pltpu.SMEM, pltpu.VMEM, pltpu.HBM))


def sizes(queries, pos):
    per_device, slots = pos.shape
    wide = (queries.shape[1] // DH) * BLOCK
    flops = 2 * slots * per_device * wide * BLOCK * DH
    return per_device, slots, (slots - 1) // 2, wide, flops


def forward(heads, slots, holder, queries, cotangent, gain, gathered):
    per_device, count, pairs, wide, flops = sizes(queries, slots)
    smem, vmem, hbm = specs()
    gathered = [pltpu.with_memory_space_constraint(g, pltpu.HBM) for g in gathered]
    return pl.pallas_call(
        lambda *refs: forward_kernel(pairs, 1.0 / math.sqrt(DH), math.log(BLOCK * count), *refs),
        out_shape=(
            jax.ShapeDtypeStruct((per_device, DH, wide), F32),
            jax.ShapeDtypeStruct((per_device, count * BLOCK, wide), F32),
            jax.ShapeDtypeStruct(((per_device * count + 1) * BLOCK, 2 * DH), BF16),
            jax.ShapeDtypeStruct((heads, 2 * per_device, BLOCK), F32),
        ),
        in_specs=[smem, smem, vmem, vmem, vmem] + [hbm] * len(GATHERED),
        out_specs=(vmem,) * 4,
        scratch_shapes=[pltpu.SemaphoreType.DMA((per_device * count,))],
        compiler_params=pltpu.CompilerParams(vmem_limit_bytes=8 << 20),
        cost_estimate=pl.CostEstimate(flops=2 * flops, bytes_accessed=16 << 20, transcendentals=0),
        name="forward",
    )(slots, holder, queries, cotangent, gain, *gathered)


def backward(heads, slots, holder, sums, queries, cotangent, gain, attended, weights, held):
    per_device, count, pairs, wide, flops = sizes(queries, slots)
    smem, vmem, hbm = specs()
    columns = float(queries.shape[1] * heads)
    grads = jax.ShapeDtypeStruct(queries.shape, BF16)
    return pl.pallas_call(
        lambda *refs: backward_kernel(pairs, 1.0 / math.sqrt(DH), columns, *refs),
        out_shape=(grads, grads)
        + tuple(jax.ShapeDtypeStruct((n * PART, 2 * DH), BF16) for n in SENT),
        in_specs=[smem, smem] + [vmem] * 7,
        out_specs=(vmem, vmem) + (hbm,) * len(SENT),
        scratch_shapes=[
            pltpu.VMEM(((per_device * count + 1) * BLOCK, 2 * DH), F32),
            pltpu.VMEM((per_device * count * BLOCK, 2 * DH), BF16),
            pltpu.VMEM((BLOCK, 2 * DH), BF16),
            pltpu.SemaphoreType.DMA((2,)),
        ],
        compiler_params=pltpu.CompilerParams(vmem_limit_bytes=14 << 20),
        cost_estimate=pl.CostEstimate(flops=5 * flops, bytes_accessed=32 << 20, transcendentals=0),
        name="backward",
    )(slots, holder, sums, queries, cotangent, gain, attended, weights, held)


def body(queries, keys, values, cotangent, gain, key_blocks, span_order):
    key_width = keys.shape[1]
    heads = lax.axis_size(HEAD)
    gain = gain.reshape(1, queries.shape[1])
    gathered = gather_blocks(jnp.concatenate([keys, values], axis=1))
    slots, source_of, back_of = positions(key_blocks, span_order, queries.shape[0] // BLOCK)
    attended, weights, held, sums = forward(
        heads, slots, source_of, queries, cotangent, gain, gathered
    )
    sums = head_copies(sums)
    output, query_grad, *parts = backward(
        heads, slots, back_of, sums, queries, cotangent, gain, attended, weights, held
    )
    grads = scatter_blocks(*parts).astype(BF16)
    return output, query_grad, grads[:, :key_width], grads[:, key_width:]


def solution(mesh):
    fine = Mesh(mesh.devices.reshape(NZ, 2, 2, 4, 2), CTX + HEAD)
    tok = P(CTX, HEAD)
    return jax.shard_map(
        body,
        mesh=fine,
        in_specs=(tok, tok, tok, tok, P(HEAD), P(), P()),
        out_specs=(tok, tok, tok, tok),
        check_vma=False,
    )
```

```python
import math

import jax
import jax.numpy as jnp
from jax import lax
from jax.experimental import pallas as pl
from jax.experimental.pallas import tpu as pltpu
from jax.sharding import Mesh, PartitionSpec as P


DH = 128
BLOCK = 128
CTX = ("z", "xh", "core")
HEAD = ("y", "xl")
RING = ("z", "core")
NZ = 16
HALF = NZ // 2
SWAP = [(0, 1), (1, 0)]
NBLK = 128
PART = 4 * BLOCK
SWAP_AFTER = (2, 4, 6, 7)
GATHERED = [1] * 16 + [4, 4, 4, 2, 1, 1]
SENT = [16, 6, 4, 4, 1, 1]
F32 = jnp.float32
BF16 = jnp.bfloat16


def ring_pairs():
    return [
        (z * 2 + c, ((z + (1 if c == 0 else -1)) % NZ) * 2 + c) for z in range(NZ) for c in range(2)
    ]


def ring(x):
    return lax.ppermute(x, RING, ring_pairs())


def swap(x):
    return lax.ppermute(x, "core", SWAP)


def gather_blocks(kv):
    pair = jnp.concatenate([kv, lax.ppermute(kv, "xh", SWAP)], axis=0)
    own, other = pair, swap(pair)
    chunk, mine, theirs = [own, other], [], []
    waiting = []
    for s in range(1, HALF):
        own, other = ring(own), ring(other)
        mine += [own, other]
        waiting += [other, own]
        if s in SWAP_AFTER:
            theirs.append(swap(jnp.concatenate(waiting, axis=0)))
            waiting = []
    return chunk + mine + theirs + [ring(own), ring(other)]


def total(*terms):
    out = terms[0].astype(F32)
    for t in terms[1:]:
        out = out + t.astype(F32)
    return out


def part_of(array, i):
    return array[i * PART : (i + 1) * PART]


def scatter_blocks(mine, near, middle, distant, *far):
    own, other = far
    near, middle, distant = swap(near), swap(middle), swap(distant)
    for s in range(HALF - 1, 0, -1):
        theirs, base = (distant, 6) if s > 5 else (middle, 4) if s > 3 else (near, 1)
        i = 2 * (s - base)
        other = ring(other)
        other = total(other, part_of(mine, 2 * s + 1), part_of(theirs, i)).astype(BF16)
        other, later_mine, later_theirs = lax.optimization_barrier((other, mine, theirs))
        own = ring(own)
        own = total(own, part_of(later_mine, 2 * s), part_of(later_theirs, i + 1)).astype(BF16)
    other = total(ring(other), part_of(mine, 1)).astype(BF16)
    own = ring(own)
    keep = total(own, part_of(mine, 0), swap(other))
    rows = PART // 2
    mate = lax.ppermute(keep[rows:].astype(BF16), "xh", SWAP)
    return keep[:rows] + mate.astype(F32)


def head_copies(x):
    return lax.all_to_all(x, HEAD, 0, 0, tiled=True)


def positions(key_blocks, span_order, per_device):
    z, xh, core = (lax.axis_index(n) for n in CTX)
    me = (z * 2 + xh) * 2 + core
    seq = lax.dynamic_slice(span_order, (me * per_device,), (per_device,))
    pick = (seq[:, None] == jnp.arange(NBLK)[None, :]).astype(jnp.int32)
    far = jnp.sum(pick[:, :, None] * key_blocks[None], axis=1)
    where = jnp.arange(NBLK, dtype=jnp.int32)
    store = jnp.sum(
        jnp.where(far[:, :, None] == span_order[None, None, :], where[None, None, :], 0), axis=2
    )
    own = me * per_device + jnp.arange(per_device, dtype=jnp.int32)
    store = jnp.concatenate([own[:, None], store], axis=1)
    live = jnp.concatenate([jnp.ones((per_device, 1), bool), far >= 0], axis=1)
    owner, half = store // per_device, store % per_device
    oz, oxh, ocore = owner // 4, (owner // 2) % 2, owner % 2
    dz = (oz - z + HALF) % NZ - HALF
    inner = (oxh ^ xh) * 2 + half
    dist = jnp.abs(dz)

    across = ocore ^ core

    def locate(first_group):
        chunk = jnp.where(first_group, 0, 14) + 2 * dist
        chunk = jnp.where(dist == 0, 0, jnp.where(dist == HALF, 30, chunk))
        return jnp.where(live, (chunk + across) * 4 + inner, NBLK).reshape(-1)

    def holder(spot):
        match = spot[None, :] == jnp.arange(NBLK, dtype=jnp.int32)[:, None]
        return jnp.max(jnp.where(match, slot[None, :], -1), axis=1)

    source = locate((dz < 0) == (core == 0))
    count = source.shape[0]
    order = jnp.arange(count, dtype=jnp.int32)
    same = source[:, None] == source[None, :]
    first = jnp.min(jnp.where(same, order[None, :], count), axis=1)
    slot = jnp.where(source == NBLK, count, first).astype(jnp.int32)
    back = locate((dz > 0) == (core == 0))
    return slot.reshape(per_device, -1), holder(source), holder(back)


def rows_of(spot):
    return pl.ds(pl.multiple_of(spot * BLOCK, BLOCK), BLOCK)


def contract_first(a, b):
    return lax.dot_general(a, b, (((0,), (0,)), ((), ())), preferred_element_type=F32)


def dot(a, b):
    return jnp.dot(a, b, preferred_element_type=F32)


def heads_of(ref, q, n):
    return [ref[pl.ds(q * BLOCK, BLOCK), h * DH : (h + 1) * DH] for h in range(n)]


def each_block(counts, visit):
    base = 0
    for k, n in enumerate(counts):

        def one(i, carry, k=k, base=base):
            visit(k, i, base + i)
            return carry

        lax.fori_loop(0, 4 * n, one, 0)
        base += 4 * n


def steps_at(i):
    if isinstance(i, int) and i == 0:
        return 0, BLOCK
    return pl.multiple_of(BLOCK + 2 * BLOCK * (i - 1), BLOCK), 2 * BLOCK


def causal_mask(width):
    key = lax.broadcasted_iota(jnp.int32, (BLOCK, width), 0)
    row = lax.broadcasted_iota(jnp.int32, (BLOCK, width), 1) % BLOCK
    return key <= row


def forward_kernel(pairs, scale, shift, slots, holder, queries, cotangent, gain, *rest):
    n = len(GATHERED)
    sources, (attended, weights, held, sums, sems) = rest[:n], rest[n:]
    per_device = slots.shape[0]
    spare = per_device * slots.shape[1]
    group = queries.shape[1] // DH
    width = group * BLOCK

    def fetch(k, i, at):
        @pl.when(holder[at] >= 0)
        def _():
            pltpu.make_async_copy(
                sources[k].at[rows_of(i), :], held.at[rows_of(holder[at]), :], sems.at[holder[at]]
            ).start()

    def await_slot(q, j):
        mine = slots[q, j]

        @pl.when(mine == q * slots.shape[1] + j)
        def _():
            pltpu.make_async_copy(
                sources[0].at[:BLOCK, :], held.at[rows_of(mine), :], sems.at[mine]
            ).wait()

        return held[rows_of(mine), :]

    each_block(GATHERED, fetch)
    held[spare * BLOCK :, :] = jnp.zeros((BLOCK, 2 * DH), BF16)
    query_t = [
        jnp.concatenate([x.T for x in heads_of(queries, q, group)], axis=1)
        for q in range(per_device)
    ]

    def weigh(keys, query):
        score = dot(keys, query)
        return 1.0 / (1.0 + jnp.exp(shift - score * scale))

    for q in range(per_device):
        own = await_slot(q, 0)
        weight = jnp.where(causal_mask(width), weigh(own[:, :DH], query_t[q]), 0.0)
        weights[q, :BLOCK, :] = weight
        attended[q] = contract_first(own[:, DH:], weight.astype(BF16))

        def step(i, carry):
            two = jnp.concatenate([await_slot(q, 1 + 2 * i), await_slot(q, 2 + 2 * i)], axis=0)
            weight = weigh(two[:, :DH], query_t[q])
            weights[q, pl.ds(*steps_at(i + 1)), :] = weight
            attended[q] += contract_first(two[:, DH:], weight.astype(BF16))
            return carry

        lax.fori_loop(0, pairs, step, 0, unroll=True)
        att = attended[q]
        grad_in = jnp.concatenate(
            [
                (x.astype(F32) * gain[:, h * DH : (h + 1) * DH]).T
                for h, x in enumerate(heads_of(cotangent, q, group))
            ],
            axis=1,
        )
        for i, value in enumerate((att * att, grad_in * att)):
            col = jnp.sum(value, axis=0, keepdims=True)
            row = col[:, :BLOCK]
            for h in range(1, group):
                row = row + col[:, h * BLOCK : (h + 1) * BLOCK]
            sums[:, 2 * q + i : 2 * q + i + 1, :] = jnp.broadcast_to(
                row[None], (sums.shape[0], 1, BLOCK)
            )


def backward_kernel(
    pairs, scale, columns, slots, holder, sums, queries, cotangent, gain, attended, weights, held, *rest
):
    m = len(SENT)
    output, query_grad = rest[:2]
    parts = rest[2 : m + 2]
    acc = rest[m + 2]
    per_device, count = slots.shape
    group = queries.shape[1] // DH
    for part in parts:
        part[...] = jnp.zeros(part.shape, BF16)
    grads_t, grads, stacked = [], [], []
    for q in range(per_device):
        inverse = lax.rsqrt(jnp.sum(sums[:, 2 * q, :], axis=0, keepdims=True) / columns + 1e-6)
        inner = jnp.sum(sums[:, 2 * q + 1, :], axis=0, keepdims=True) / columns
        back = inverse * inverse * inner
        grad_t, grad = [], []
        for h, x in enumerate(heads_of(cotangent, q, group)):
            gain_h = gain[:, h * DH : (h + 1) * DH]
            att = attended[q, :, h * BLOCK : (h + 1) * BLOCK]
            grad_in = (x.astype(F32) * gain_h).T
            low = inverse * (grad_in - att * back)
            grad_t.append(low.astype(BF16))
            grad.append(low.T.astype(BF16))
            output[pl.ds(q * BLOCK, BLOCK), h * DH : (h + 1) * DH] = (
                (att * inverse).T * gain_h
            ).astype(BF16)
        grads_t.append(jnp.concatenate(grad_t, axis=1))
        grads.append(jnp.concatenate(grad, axis=0))
        stacked.append(jnp.concatenate(heads_of(queries, q, group), axis=0))

    def pair_grads(q, both, weight):
        low = weight.astype(BF16)
        grad_weight = dot(both[:, DH:], grads_t[q])
        grad_score = (grad_weight * (weight * (1.0 - weight))).astype(BF16)
        part = jnp.concatenate([dot(grad_score, stacked[q]) * scale, dot(low, grads[q])], axis=1)
        return contract_first(both[:, :DH], grad_score), part

    def keep_part(q, j, part):
        slot = slots[q, j]
        if q > 0:
            again = slot < q * count
            part = part + jnp.where(again, acc[rows_of(slot), :], 0.0)
        acc[rows_of(slot), :] = part

    for q in range(per_device):
        own = held[rows_of(slots[q, 0]), :]
        query_part, part = pair_grads(q, own, weights[q, :BLOCK, :])
        keep_part(q, 0, part)

        def step(i, query_part):
            two = jnp.concatenate(
                [held[rows_of(slots[q, 1 + 2 * i]), :], held[rows_of(slots[q, 2 + 2 * i]), :]], axis=0
            )
            more, part = pair_grads(q, two, weights[q, pl.ds(*steps_at(i + 1)), :])
            keep_part(q, 1 + 2 * i, part[:BLOCK])
            keep_part(q, 2 + 2 * i, part[BLOCK:])
            return query_part + more

        query_part = lax.fori_loop(0, pairs, step, query_part, unroll=True)
        for h in range(group):
            query_grad[pl.ds(q * BLOCK, BLOCK), h * DH : (h + 1) * DH] = (
                query_part[:, h * BLOCK : (h + 1) * BLOCK].T * scale
            ).astype(BF16)

    def hand_over(k, i, at):
        @pl.when(holder[at] >= 0)
        def _():
            parts[k][rows_of(i), :] = acc[rows_of(holder[at]), :].astype(BF16)

    each_block(SENT, hand_over)


def specs():
    return tuple(pl.BlockSpec(memory_space=m) for m in (pltpu.SMEM, pltpu.VMEM, pltpu.HBM))


def sizes(queries, pos):
    per_device, slots = pos.shape
    wide = (queries.shape[1] // DH) * BLOCK
    flops = 2 * slots * per_device * wide * BLOCK * DH
    return per_device, slots, (slots - 1) // 2, wide, flops


def forward(heads, slots, holder, queries, cotangent, gain, gathered):
    per_device, count, pairs, wide, flops = sizes(queries, slots)
    smem, vmem, hbm = specs()
    gathered = [pltpu.with_memory_space_constraint(g, pltpu.HBM) for g in gathered]
    return pl.pallas_call(
        lambda *refs: forward_kernel(pairs, 1.0 / math.sqrt(DH), math.log(BLOCK * count), *refs),
        out_shape=(
            jax.ShapeDtypeStruct((per_device, DH, wide), F32),
            jax.ShapeDtypeStruct((per_device, count * BLOCK, wide), F32),
            jax.ShapeDtypeStruct(((per_device * count + 1) * BLOCK, 2 * DH), BF16),
            jax.ShapeDtypeStruct((heads, 2 * per_device, BLOCK), F32),
        ),
        in_specs=[smem, smem, vmem, vmem, vmem] + [hbm] * len(GATHERED),
        out_specs=(vmem,) * 4,
        scratch_shapes=[pltpu.SemaphoreType.DMA((per_device * count,))],
        compiler_params=pltpu.CompilerParams(vmem_limit_bytes=8 << 20),
        cost_estimate=pl.CostEstimate(flops=2 * flops, bytes_accessed=16 << 20, transcendentals=0),
        name="forward",
    )(slots, holder, queries, cotangent, gain, *gathered)


def backward(heads, slots, holder, sums, queries, cotangent, gain, attended, weights, held):
    per_device, count, pairs, _, flops = sizes(queries, slots)
    smem, vmem, _ = specs()
    columns = float(queries.shape[1] * heads)
    grads = jax.ShapeDtypeStruct(queries.shape, BF16)
    return pl.pallas_call(
        lambda *refs: backward_kernel(pairs, 1.0 / math.sqrt(DH), columns, *refs),
        out_shape=(grads, grads)
        + tuple(jax.ShapeDtypeStruct((n * PART, 2 * DH), BF16) for n in SENT),
        in_specs=[smem, smem] + [vmem] * 7,
        out_specs=(vmem,) * (2 + len(SENT)),
        scratch_shapes=[
            pltpu.VMEM(((per_device * count + 1) * BLOCK, 2 * DH), F32),
        ],
        compiler_params=pltpu.CompilerParams(vmem_limit_bytes=14 << 20),
        cost_estimate=pl.CostEstimate(flops=5 * flops, bytes_accessed=32 << 20, transcendentals=0),
        name="backward",
    )(slots, holder, sums, queries, cotangent, gain, attended, weights, held)


def body(queries, keys, values, cotangent, gain, key_blocks, span_order):
    key_width = keys.shape[1]
    heads = lax.axis_size(HEAD)
    gain = gain.reshape(1, queries.shape[1])
    gathered = gather_blocks(jnp.concatenate([keys, values], axis=1))
    slots, source_of, back_of = positions(key_blocks, span_order, queries.shape[0] // BLOCK)
    attended, weights, held, sums = forward(
        heads, slots, source_of, queries, cotangent, gain, gathered
    )
    sums = head_copies(sums)
    output, query_grad, *parts = backward(
        heads, slots, back_of, sums, queries, cotangent, gain, attended, weights, held
    )
    grads = scatter_blocks(*parts).astype(BF16)
    return output, query_grad, grads[:, :key_width], grads[:, key_width:]


def solution(mesh):
    fine = Mesh(mesh.devices.reshape(NZ, 2, 2, 4, 2), CTX + HEAD)
    tok = P(CTX, HEAD)
    return jax.shard_map(
        body,
        mesh=fine,
        in_specs=(tok, tok, tok, tok, P(HEAD), P(), P()),
        out_specs=(tok, tok, tok, tok),
        check_vma=False,
    )
```

```python
import math

import jax
import jax.numpy as jnp
from jax import lax
from jax.experimental import pallas as pl
from jax.experimental.pallas import tpu as pltpu
from jax.sharding import Mesh, PartitionSpec as P


DH = 128
BLOCK = 128
CTX = ("z", "xh", "core")
HEAD = ("y", "xl")
RING = ("z", "core")
NZ = 16
HALF = NZ // 2
SWAP = [(0, 1), (1, 0)]
NBLK = 128
PART = 4 * BLOCK
SWAP_AFTER = (2, 4, 6, 7)
GATHERED = [1] * 16 + [4, 4, 4, 2, 1, 1]
SENT = [16, 6, 4, 4, 1, 1]
F32 = jnp.float32
BF16 = jnp.bfloat16


def ring_pairs():
    return [
        (z * 2 + c, ((z + (1 if c == 0 else -1)) % NZ) * 2 + c) for z in range(NZ) for c in range(2)
    ]


def ring(x):
    return lax.ppermute(x, RING, ring_pairs())


def swap(x):
    return lax.ppermute(x, "core", SWAP)


def gather_blocks(kv):
    pair = jnp.concatenate([kv, lax.ppermute(kv, "xh", SWAP)], axis=0)
    own, other = pair, swap(pair)
    chunk, mine, theirs = [own, other], [], []
    waiting = []
    for s in range(1, HALF):
        own, other = ring(own), ring(other)
        mine += [own, other]
        waiting += [other, own]
        if s in SWAP_AFTER:
            theirs.append(swap(jnp.concatenate(waiting, axis=0)))
            waiting = []
    return chunk + mine + theirs + [ring(own), ring(other)]


def total(*terms):
    out = terms[0].astype(F32)
    for t in terms[1:]:
        out = out + t.astype(F32)
    return out


def part_of(array, i):
    return array[i * PART : (i + 1) * PART]


def scatter_blocks(mine, near, middle, distant, *far):
    own, other = far
    near, middle, distant = swap(near), swap(middle), swap(distant)
    for s in range(HALF - 1, 0, -1):
        theirs, base = (distant, 6) if s > 5 else (middle, 4) if s > 3 else (near, 1)
        i = 2 * (s - base)
        other = ring(other)
        other = total(other, part_of(mine, 2 * s + 1), part_of(theirs, i)).astype(BF16)
        other, later_mine, later_theirs = lax.optimization_barrier((other, mine, theirs))
        own = ring(own)
        own = total(own, part_of(later_mine, 2 * s), part_of(later_theirs, i + 1)).astype(BF16)
    rows = PART // 2
    other = total(ring(other), part_of(mine, 1)).astype(BF16)
    other, mine = lax.optimization_barrier((other, mine))
    across = lax.ppermute(other[rows:], ("xh", "core"), [(i, 3 - i) for i in range(4)])
    near_core = swap(other[:rows])
    own = total(ring(own), part_of(mine, 0))
    mate = lax.ppermute(own[rows:].astype(BF16), "xh", SWAP)
    return total(own[:rows], near_core, across, mate)


def head_copies(x):
    return lax.all_to_all(x, HEAD, 0, 0, tiled=True)


def positions(key_blocks, span_order, per_device):
    z, xh, core = (lax.axis_index(n) for n in CTX)
    me = (z * 2 + xh) * 2 + core
    seq = lax.dynamic_slice(span_order, (me * per_device,), (per_device,))
    pick = (seq[:, None] == jnp.arange(NBLK)[None, :]).astype(jnp.int32)
    far = jnp.sum(pick[:, :, None] * key_blocks[None], axis=1)
    where = jnp.arange(NBLK, dtype=jnp.int32)
    store = jnp.sum(
        jnp.where(far[:, :, None] == span_order[None, None, :], where[None, None, :], 0), axis=2
    )
    own = me * per_device + jnp.arange(per_device, dtype=jnp.int32)
    store = jnp.concatenate([own[:, None], store], axis=1)
    live = jnp.concatenate([jnp.ones((per_device, 1), bool), far >= 0], axis=1)
    owner, half = store // per_device, store % per_device
    oz, oxh, ocore = owner // 4, (owner // 2) % 2, owner % 2
    dz = (oz - z + HALF) % NZ - HALF
    inner = (oxh ^ xh) * 2 + half
    dist = jnp.abs(dz)

    across = ocore ^ core

    def locate(first_group):
        chunk = jnp.where(first_group, 0, 14) + 2 * dist
        chunk = jnp.where(dist == 0, 0, jnp.where(dist == HALF, 30, chunk))
        return jnp.where(live, (chunk + across) * 4 + inner, NBLK).reshape(-1)

    def holder(spot):
        match = spot[None, :] == jnp.arange(NBLK, dtype=jnp.int32)[:, None]
        return jnp.max(jnp.where(match, slot[None, :], -1), axis=1)

    source = locate((dz < 0) == (core == 0))
    count = source.shape[0]
    order = jnp.arange(count, dtype=jnp.int32)
    same = source[:, None] == source[None, :]
    first = jnp.min(jnp.where(same, order[None, :], count), axis=1)
    slot = jnp.where(source == NBLK, count, first).astype(jnp.int32)
    back = locate((dz > 0) == (core == 0))
    return slot.reshape(per_device, -1), holder(source), holder(back)


def rows_of(spot):
    return pl.ds(pl.multiple_of(spot * BLOCK, BLOCK), BLOCK)


def contract_first(a, b):
    return lax.dot_general(a, b, (((0,), (0,)), ((), ())), preferred_element_type=F32)


def dot(a, b):
    return jnp.dot(a, b, preferred_element_type=F32)


def heads_of(ref, q, n):
    return [ref[pl.ds(q * BLOCK, BLOCK), h * DH : (h + 1) * DH] for h in range(n)]


def each_block(counts, visit):
    base = 0
    for k, n in enumerate(counts):

        def one(i, carry, k=k, base=base):
            visit(k, i, base + i)
            return carry

        lax.fori_loop(0, 4 * n, one, 0)
        base += 4 * n


def steps_at(i):
    if isinstance(i, int) and i == 0:
        return 0, BLOCK
    return pl.multiple_of(BLOCK + 2 * BLOCK * (i - 1), BLOCK), 2 * BLOCK


def causal_mask(width):
    key = lax.broadcasted_iota(jnp.int32, (BLOCK, width), 0)
    row = lax.broadcasted_iota(jnp.int32, (BLOCK, width), 1) % BLOCK
    return key <= row


def forward_kernel(pairs, scale, shift, slots, holder, queries, cotangent, gain, *rest):
    n = len(GATHERED)
    sources, (attended, weights, held, sums, sems) = rest[:n], rest[n:]
    per_device = slots.shape[0]
    spare = per_device * slots.shape[1]
    group = queries.shape[1] // DH
    width = group * BLOCK

    def fetch(k, i, at):
        @pl.when(holder[at] >= 0)
        def _():
            pltpu.make_async_copy(
                sources[k].at[rows_of(i), :], held.at[rows_of(holder[at]), :], sems.at[holder[at]]
            ).start()

    def await_slot(q, j):
        mine = slots[q, j]

        @pl.when(mine == q * slots.shape[1] + j)
        def _():
            pltpu.make_async_copy(
                sources[0].at[:BLOCK, :], held.at[rows_of(mine), :], sems.at[mine]
            ).wait()

        return held[rows_of(mine), :]

    each_block(GATHERED, fetch)
    held[spare * BLOCK :, :] = jnp.zeros((BLOCK, 2 * DH), BF16)
    query_t = [
        jnp.concatenate([x.T for x in heads_of(queries, q, group)], axis=1)
        for q in range(per_device)
    ]

    def weigh(keys, query):
        score = dot(keys, query)
        return 1.0 / (1.0 + jnp.exp(shift - score * scale))

    for q in range(per_device):
        own = await_slot(q, 0)
        weight = jnp.where(causal_mask(width), weigh(own[:, :DH], query_t[q]), 0.0)
        weights[q, :BLOCK, :] = weight
        attended[q] = contract_first(own[:, DH:], weight.astype(BF16))

        def step(i, carry):
            two = jnp.concatenate([await_slot(q, 1 + 2 * i), await_slot(q, 2 + 2 * i)], axis=0)
            weight = weigh(two[:, :DH], query_t[q])
            weights[q, pl.ds(*steps_at(i + 1)), :] = weight
            attended[q] += contract_first(two[:, DH:], weight.astype(BF16))
            return carry

        lax.fori_loop(0, pairs, step, 0, unroll=True)
        att = attended[q]
        grad_in = jnp.concatenate(
            [
                (x.astype(F32) * gain[:, h * DH : (h + 1) * DH]).T
                for h, x in enumerate(heads_of(cotangent, q, group))
            ],
            axis=1,
        )
        for i, value in enumerate((att * att, grad_in * att)):
            col = jnp.sum(value, axis=0, keepdims=True)
            row = col[:, :BLOCK]
            for h in range(1, group):
                row = row + col[:, h * BLOCK : (h + 1) * BLOCK]
            sums[:, 2 * q + i : 2 * q + i + 1, :] = jnp.broadcast_to(
                row[None], (sums.shape[0], 1, BLOCK)
            )


def row_terms(q, columns, sums):
    squares = jnp.sum(sums[:, 2 * q, :], axis=0, keepdims=True)
    crossed = jnp.sum(sums[:, 2 * q + 1, :], axis=0, keepdims=True)
    return lax.rsqrt(squares / columns + 1e-6), crossed / columns


def backward_kernel(
    pairs, scale, columns, slots, holder, sums, queries, cotangent, gain, attended, weights, held, *rest
):
    scores, parts, acc = rest[0], rest[1:-1], rest[-1]
    per_device, count = slots.shape
    group = queries.shape[1] // DH
    for part in parts:
        part[...] = jnp.zeros(part.shape, BF16)
    grads_t, grads, stacked = [], [], []
    for q in range(per_device):
        inverse, inner = row_terms(q, columns, sums)
        back = inverse * inverse * inner
        grad_t, grad = [], []
        for h, x in enumerate(heads_of(cotangent, q, group)):
            gain_h = gain[:, h * DH : (h + 1) * DH]
            att = attended[q, :, h * BLOCK : (h + 1) * BLOCK]
            grad_in = (x.astype(F32) * gain_h).T
            low = inverse * (grad_in - att * back)
            grad_t.append(low.astype(BF16))
            grad.append(low.T.astype(BF16))
        grads_t.append(jnp.concatenate(grad_t, axis=1))
        grads.append(jnp.concatenate(grad, axis=0))
        stacked.append(jnp.concatenate(heads_of(queries, q, group), axis=0))

    def pair_grads(q, both, span):
        weight = weights[q, span, :]
        grad_weight = dot(both[:, DH:], grads_t[q])
        grad_score = (grad_weight * (weight * (1.0 - weight))).astype(BF16)
        scores[q, span, :] = grad_score
        low = weight.astype(BF16)
        return jnp.concatenate([dot(grad_score, stacked[q]) * scale, dot(low, grads[q])], axis=1)

    def keep_part(q, j, part):
        slot = slots[q, j]
        if q > 0:
            again = slot < q * count
            part = part + jnp.where(again, acc[rows_of(slot), :], 0.0)
        acc[rows_of(slot), :] = part

    for q in range(per_device):
        keep_part(q, 0, pair_grads(q, held[rows_of(slots[q, 0]), :], pl.ds(0, BLOCK)))

        def step(i, carry):
            part = pair_grads(q, pair_of(held, slots, q, i), pl.ds(*steps_at(i + 1)))
            keep_part(q, 1 + 2 * i, part[:BLOCK])
            keep_part(q, 2 + 2 * i, part[BLOCK:])
            return carry

        lax.fori_loop(0, pairs, step, 0, unroll=True)

    def hand_over(k, i, at):
        @pl.when(holder[at] >= 0)
        def _():
            parts[k][rows_of(i), :] = acc[rows_of(holder[at]), :].astype(BF16)

    each_block(SENT, hand_over)


def pair_of(held, slots, q, i):
    return jnp.concatenate(
        [held[rows_of(slots[q, 1 + 2 * i]), :], held[rows_of(slots[q, 2 + 2 * i]), :]], axis=0
    )


def finish_kernel(
    pairs, scale, columns, slots, sums, gain, attended, scores, held, output, query_grad
):
    per_device = slots.shape[0]
    group = output.shape[1] // DH
    for q in range(per_device):
        rows = pl.ds(q * BLOCK, BLOCK)
        inverse, _ = row_terms(q, columns, sums)
        for h in range(group):
            span = slice(h * DH, (h + 1) * DH)
            att = attended[q, :, h * BLOCK : (h + 1) * BLOCK]
            output[rows, span] = ((att * inverse).T * gain[:, span]).astype(BF16)
        grad = contract_first(held[rows_of(slots[q, 0]), :DH], scores[q, :BLOCK, :])

        def step(i, grad):
            two = pair_of(held, slots, q, i)[:, :DH]
            return grad + contract_first(two, scores[q, pl.ds(*steps_at(i + 1)), :])

        grad = lax.fori_loop(0, pairs, step, grad, unroll=True)
        for h in range(group):
            query_grad[rows, h * DH : (h + 1) * DH] = (
                grad[:, h * BLOCK : (h + 1) * BLOCK].T * scale
            ).astype(BF16)


def specs():
    return tuple(pl.BlockSpec(memory_space=m) for m in (pltpu.SMEM, pltpu.VMEM, pltpu.HBM))


def sizes(queries, pos):
    per_device, slots = pos.shape
    wide = (queries.shape[1] // DH) * BLOCK
    flops = 2 * slots * per_device * wide * BLOCK * DH
    return per_device, slots, (slots - 1) // 2, wide, flops


def forward(heads, slots, holder, queries, cotangent, gain, gathered):
    per_device, count, pairs, wide, flops = sizes(queries, slots)
    smem, vmem, hbm = specs()
    gathered = [pltpu.with_memory_space_constraint(g, pltpu.HBM) for g in gathered]
    return pl.pallas_call(
        lambda *refs: forward_kernel(pairs, 1.0 / math.sqrt(DH), math.log(BLOCK * count), *refs),
        out_shape=(
            jax.ShapeDtypeStruct((per_device, DH, wide), F32),
            jax.ShapeDtypeStruct((per_device, count * BLOCK, wide), F32),
            jax.ShapeDtypeStruct(((per_device * count + 1) * BLOCK, 2 * DH), BF16),
            jax.ShapeDtypeStruct((heads, 2 * per_device, BLOCK), F32),
        ),
        in_specs=[smem, smem, vmem, vmem, vmem] + [hbm] * len(GATHERED),
        out_specs=(vmem,) * 4,
        scratch_shapes=[pltpu.SemaphoreType.DMA((per_device * count,))],
        compiler_params=pltpu.CompilerParams(vmem_limit_bytes=8 << 20),
        cost_estimate=pl.CostEstimate(flops=2 * flops, bytes_accessed=16 << 20, transcendentals=0),
        name="forward",
    )(slots, holder, queries, cotangent, gain, *gathered)


def backward(heads, slots, holder, sums, queries, cotangent, gain, attended, weights, held):
    per_device, count, pairs, wide, flops = sizes(queries, slots)
    smem, vmem, _ = specs()
    columns = float(queries.shape[1] * heads)
    return pl.pallas_call(
        lambda *refs: backward_kernel(pairs, 1.0 / math.sqrt(DH), columns, *refs),
        out_shape=(jax.ShapeDtypeStruct((per_device, count * BLOCK, wide), BF16),)
        + tuple(jax.ShapeDtypeStruct((n * PART, 2 * DH), BF16) for n in SENT),
        in_specs=[smem, smem] + [vmem] * 7,
        out_specs=(vmem,) * (1 + len(SENT)),
        scratch_shapes=[pltpu.VMEM(((per_device * count + 1) * BLOCK, 2 * DH), F32)],
        compiler_params=pltpu.CompilerParams(vmem_limit_bytes=14 << 20),
        cost_estimate=pl.CostEstimate(flops=3 * flops, bytes_accessed=32 << 20, transcendentals=0),
        name="backward",
    )(slots, holder, sums, queries, cotangent, gain, attended, weights, held)


def finish(heads, slots, sums, gain, attended, scores, held):
    per_device, count, pairs, wide, _ = sizes(gain, slots)
    smem, vmem, _ = specs()
    width = gain.shape[1]
    grads = jax.ShapeDtypeStruct((per_device * BLOCK, width), BF16)
    flops = 2 * count * per_device * wide * BLOCK * DH
    return pl.pallas_call(
        lambda *refs: finish_kernel(pairs, 1.0 / math.sqrt(DH), float(width * heads), *refs),
        out_shape=(grads, grads),
        in_specs=[smem] + [vmem] * 5,
        out_specs=(vmem, vmem),
        compiler_params=pltpu.CompilerParams(vmem_limit_bytes=8 << 20),
        cost_estimate=pl.CostEstimate(flops=flops, bytes_accessed=8 << 20, transcendentals=0),
        name="finish",
    )(slots, sums, gain, attended, scores, held)


def body(queries, keys, values, cotangent, gain, key_blocks, span_order):
    key_width = keys.shape[1]
    heads = lax.axis_size(HEAD)
    gain = gain.reshape(1, queries.shape[1])
    gathered = gather_blocks(jnp.concatenate([keys, values], axis=1))
    slots, source_of, back_of = positions(key_blocks, span_order, queries.shape[0] // BLOCK)
    attended, weights, held, sums = forward(
        heads, slots, source_of, queries, cotangent, gain, gathered
    )
    sums = head_copies(sums)
    scores, *parts = backward(
        heads, slots, back_of, sums, queries, cotangent, gain, attended, weights, held
    )
    grads = scatter_blocks(*parts).astype(BF16)
    output, query_grad = finish(heads, slots, sums, gain, attended, scores, held)
    return output, query_grad, grads[:, :key_width], grads[:, key_width:]


def solution(mesh):
    fine = Mesh(mesh.devices.reshape(NZ, 2, 2, 4, 2), CTX + HEAD)
    tok = P(CTX, HEAD)
    return jax.shard_map(
        body,
        mesh=fine,
        in_specs=(tok, tok, tok, tok, P(HEAD), P(), P()),
        out_specs=(tok, tok, tok, tok),
        check_vma=False,
    )
```

```python
import math

import jax
import jax.numpy as jnp
from jax import lax
from jax.experimental import pallas as pl
from jax.experimental.pallas import tpu as pltpu
from jax.sharding import Mesh, PartitionSpec as P


DH = 128
BLOCK = 128
CTX = ("z", "xh", "core")
HEAD = ("y", "xl")
RING = ("z", "core")
NZ = 16
HALF = NZ // 2
SWAP = [(0, 1), (1, 0)]
NBLK = 128
PART = 4 * BLOCK
SWAP_AFTER = (2, 5, 7)
GATHERED = [1] * 16 + [4, 6, 4, 1, 1]
SENT = [16, 6, 4, 4, 1, 1]
F32 = jnp.float32
BF16 = jnp.bfloat16


def ring_pairs():
    return [
        (z * 2 + c, ((z + (1 if c == 0 else -1)) % NZ) * 2 + c) for z in range(NZ) for c in range(2)
    ]


def ring(x):
    return lax.ppermute(x, RING, ring_pairs())


def swap(x):
    return lax.ppermute(x, "core", SWAP)


def gather_blocks(kv):
    pair = jnp.concatenate([kv, lax.ppermute(kv, "xh", SWAP)], axis=0)
    own, other = pair, swap(pair)
    chunk, mine, theirs = [own, other], [], []
    waiting = []
    for s in range(1, HALF):
        own, other = ring(own), ring(other)
        mine += [own, other]
        waiting += [other, own]
        if s in SWAP_AFTER:
            theirs.append(swap(jnp.concatenate(waiting, axis=0)))
            waiting = []
    return chunk + mine + theirs + [ring(own), ring(other)]


def total(*terms):
    out = terms[0].astype(F32)
    for t in terms[1:]:
        out = out + t.astype(F32)
    return out


def part_of(array, i):
    return array[i * PART : (i + 1) * PART]


def scatter_blocks(mine, near, middle, distant, *far):
    own, other = far
    near, middle, distant = swap(near), swap(middle), swap(distant)
    for s in range(HALF - 1, 0, -1):
        theirs, base = (distant, 6) if s > 5 else (middle, 4) if s > 3 else (near, 1)
        i = 2 * (s - base)
        other = ring(other)
        other = total(other, part_of(mine, 2 * s + 1), part_of(theirs, i)).astype(BF16)
        other, later_mine, later_theirs = lax.optimization_barrier((other, mine, theirs))
        own = ring(own)
        own = total(own, part_of(later_mine, 2 * s), part_of(later_theirs, i + 1)).astype(BF16)
    rows = PART // 2
    other = total(ring(other), part_of(mine, 1)).astype(BF16)
    other, mine = lax.optimization_barrier((other, mine))
    own = ring(own)
    own = total(own, part_of(mine, 0), swap(other))
    mate = lax.ppermute(own[rows:].astype(BF16), "xh", SWAP)
    return total(own[:rows], mate)


def head_copies(x):
    return lax.all_to_all(x, HEAD, 0, 0, tiled=True)


def positions(key_blocks, span_order, per_device):
    z, xh, core = (lax.axis_index(n) for n in CTX)
    me = (z * 2 + xh) * 2 + core
    seq = lax.dynamic_slice(span_order, (me * per_device,), (per_device,))
    pick = (seq[:, None] == jnp.arange(NBLK)[None, :]).astype(jnp.int32)
    far = jnp.sum(pick[:, :, None] * key_blocks[None], axis=1)
    where = jnp.arange(NBLK, dtype=jnp.int32)
    store = jnp.sum(
        jnp.where(far[:, :, None] == span_order[None, None, :], where[None, None, :], 0), axis=2
    )
    own = me * per_device + jnp.arange(per_device, dtype=jnp.int32)
    store = jnp.concatenate([own[:, None], store], axis=1)
    live = jnp.concatenate([jnp.ones((per_device, 1), bool), far >= 0], axis=1)
    owner, half = store // per_device, store % per_device
    oz, oxh, ocore = owner // 4, (owner // 2) % 2, owner % 2
    dz = (oz - z + HALF) % NZ - HALF
    inner = (oxh ^ xh) * 2 + half
    dist = jnp.abs(dz)

    across = ocore ^ core

    def locate(first_group):
        chunk = jnp.where(first_group, 0, 14) + 2 * dist
        chunk = jnp.where(dist == 0, 0, jnp.where(dist == HALF, 30, chunk))
        return jnp.where(live, (chunk + across) * 4 + inner, NBLK).reshape(-1)

    def holder(spot):
        match = spot[None, :] == jnp.arange(NBLK, dtype=jnp.int32)[:, None]
        return jnp.max(jnp.where(match, slot[None, :], -1), axis=1)

    source = locate((dz < 0) == (core == 0))
    count = source.shape[0]
    order = jnp.arange(count, dtype=jnp.int32)
    same = source[:, None] == source[None, :]
    first = jnp.min(jnp.where(same, order[None, :], count), axis=1)
    slot = jnp.where(source == NBLK, count, first).astype(jnp.int32)
    back = locate((dz > 0) == (core == 0))
    return slot.reshape(per_device, -1), holder(source), holder(back)


def rows_of(spot):
    return pl.ds(pl.multiple_of(spot * BLOCK, BLOCK), BLOCK)


def contract_first(a, b):
    return lax.dot_general(a, b, (((0,), (0,)), ((), ())), preferred_element_type=F32)


def dot(a, b):
    return jnp.dot(a, b, preferred_element_type=F32)


def heads_of(ref, q, n):
    return [ref[pl.ds(q * BLOCK, BLOCK), h * DH : (h + 1) * DH] for h in range(n)]


def each_block(counts, visit):
    base = 0
    for k, n in enumerate(counts):

        def one(i, carry, k=k, base=base):
            visit(k, i, base + i)
            return carry

        lax.fori_loop(0, 4 * n, one, 0)
        base += 4 * n


def steps_at(i):
    if isinstance(i, int) and i == 0:
        return 0, BLOCK
    return pl.multiple_of(BLOCK + 2 * BLOCK * (i - 1), BLOCK), 2 * BLOCK


def causal_mask(width):
    key = lax.broadcasted_iota(jnp.int32, (BLOCK, width), 0)
    row = lax.broadcasted_iota(jnp.int32, (BLOCK, width), 1) % BLOCK
    return key <= row


def forward_kernel(pairs, scale, shift, slots, holder, queries, cotangent, gain, *rest):
    n = len(GATHERED)
    sources, (attended, weights, held, sums, sems) = rest[:n], rest[n:]
    per_device = slots.shape[0]
    spare = per_device * slots.shape[1]
    group = queries.shape[1] // DH
    width = group * BLOCK

    def fetch(k, i, at):
        @pl.when(holder[at] >= 0)
        def _():
            pltpu.make_async_copy(
                sources[k].at[rows_of(i), :], held.at[rows_of(holder[at]), :], sems.at[holder[at]]
            ).start()

    def await_slot(q, j):
        mine = slots[q, j]

        @pl.when(mine == q * slots.shape[1] + j)
        def _():
            pltpu.make_async_copy(
                sources[0].at[:BLOCK, :], held.at[rows_of(mine), :], sems.at[mine]
            ).wait()

        return held[rows_of(mine), :]

    each_block(GATHERED, fetch)
    held[spare * BLOCK :, :] = jnp.zeros((BLOCK, 2 * DH), BF16)
    query_t = [
        jnp.concatenate([x.T for x in heads_of(queries, q, group)], axis=1)
        for q in range(per_device)
    ]

    def weigh(keys, query):
        score = dot(keys, query)
        return 1.0 / (1.0 + jnp.exp2(shift * math.log2(math.e) - score * (scale * math.log2(math.e))))

    for q in range(per_device):
        own = await_slot(q, 0)
        weight = jnp.where(causal_mask(width), weigh(own[:, :DH], query_t[q]), 0.0)
        weights[q, :BLOCK, :] = weight
        attended[q] = contract_first(own[:, DH:], weight.astype(BF16))

        def step(i, carry):
            two = jnp.concatenate([await_slot(q, 1 + 2 * i), await_slot(q, 2 + 2 * i)], axis=0)
            weight = weigh(two[:, :DH], query_t[q])
            weights[q, pl.ds(*steps_at(i + 1)), :] = weight
            attended[q] += contract_first(two[:, DH:], weight.astype(BF16))
            return carry

        lax.fori_loop(0, pairs, step, 0, unroll=True)
        att = attended[q]
        grad_in = jnp.concatenate(
            [
                (x.astype(F32) * gain[:, h * DH : (h + 1) * DH]).T
                for h, x in enumerate(heads_of(cotangent, q, group))
            ],
            axis=1,
        )
        for i, value in enumerate((att * att, grad_in * att)):
            col = jnp.sum(value, axis=0, keepdims=True)
            row = col[:, :BLOCK]
            for h in range(1, group):
                row = row + col[:, h * BLOCK : (h + 1) * BLOCK]
            sums[:, 2 * q + i : 2 * q + i + 1, :] = jnp.broadcast_to(
                row[None], (sums.shape[0], 1, BLOCK)
            )


def row_terms(q, columns, sums):
    squares = jnp.sum(sums[:, 2 * q, :], axis=0, keepdims=True)
    crossed = jnp.sum(sums[:, 2 * q + 1, :], axis=0, keepdims=True)
    return lax.rsqrt(squares / columns + 1e-6), crossed / columns


def backward_kernel(
    pairs, scale, columns, slots, holder, sums, queries, cotangent, gain, attended, weights, held, *rest
):
    scores, parts, acc = rest[0], rest[1:-1], rest[-1]
    per_device, count = slots.shape
    group = queries.shape[1] // DH
    for part in parts:
        part[...] = jnp.zeros(part.shape, BF16)
    grads_t, grads, stacked = [], [], []
    for q in range(per_device):
        inverse, inner = row_terms(q, columns, sums)
        back = inverse * inverse * inner
        grad_t, grad = [], []
        for h, x in enumerate(heads_of(cotangent, q, group)):
            gain_h = gain[:, h * DH : (h + 1) * DH]
            att = attended[q, :, h * BLOCK : (h + 1) * BLOCK]
            grad_in = (x.astype(F32) * gain_h).T
            low = inverse * (grad_in - att * back)
            grad_t.append(low.astype(BF16))
            grad.append(low.T.astype(BF16))
        grads_t.append(jnp.concatenate(grad_t, axis=1))
        grads.append(jnp.concatenate(grad, axis=0))
        stacked.append(jnp.concatenate(heads_of(queries, q, group), axis=0))

    def pair_grads(q, both, span):
        weight = weights[q, span, :]
        grad_weight = dot(both[:, DH:], grads_t[q])
        grad_score = (grad_weight * (weight * (1.0 - weight))).astype(BF16)
        scores[q, span, :] = grad_score
        low = weight.astype(BF16)
        return jnp.concatenate([dot(grad_score, stacked[q]) * scale, dot(low, grads[q])], axis=1)

    def keep_part(q, j, part):
        slot = slots[q, j]
        if q > 0:
            again = slot < q * count
            part = part + jnp.where(again, acc[rows_of(slot), :], 0.0)
        acc[rows_of(slot), :] = part

    for q in range(per_device):
        keep_part(q, 0, pair_grads(q, held[rows_of(slots[q, 0]), :], pl.ds(0, BLOCK)))

        def step(i, carry):
            part = pair_grads(q, pair_of(held, slots, q, i), pl.ds(*steps_at(i + 1)))
            keep_part(q, 1 + 2 * i, part[:BLOCK])
            keep_part(q, 2 + 2 * i, part[BLOCK:])
            return carry

        lax.fori_loop(0, pairs, step, 0, unroll=True)

    def hand_over(k, i, at):
        @pl.when(holder[at] >= 0)
        def _():
            parts[k][rows_of(i), :] = acc[rows_of(holder[at]), :].astype(BF16)

    each_block(SENT, hand_over)


def pair_of(held, slots, q, i):
    return jnp.concatenate(
        [held[rows_of(slots[q, 1 + 2 * i]), :], held[rows_of(slots[q, 2 + 2 * i]), :]], axis=0
    )


def finish_kernel(
    pairs, scale, columns, slots, sums, gain, attended, scores, held, output, query_grad
):
    per_device = slots.shape[0]
    group = output.shape[1] // DH
    for q in range(per_device):
        rows = pl.ds(q * BLOCK, BLOCK)
        inverse, _ = row_terms(q, columns, sums)
        for h in range(group):
            span = slice(h * DH, (h + 1) * DH)
            att = attended[q, :, h * BLOCK : (h + 1) * BLOCK]
            output[rows, span] = ((att * inverse).T * gain[:, span]).astype(BF16)
        grad = contract_first(held[rows_of(slots[q, 0]), :DH], scores[q, :BLOCK, :])

        def step(i, grad):
            two = pair_of(held, slots, q, i)[:, :DH]
            return grad + contract_first(two, scores[q, pl.ds(*steps_at(i + 1)), :])

        grad = lax.fori_loop(0, pairs, step, grad, unroll=True)
        for h in range(group):
            query_grad[rows, h * DH : (h + 1) * DH] = (
                grad[:, h * BLOCK : (h + 1) * BLOCK].T * scale
            ).astype(BF16)


def specs():
    return tuple(pl.BlockSpec(memory_space=m) for m in (pltpu.SMEM, pltpu.VMEM, pltpu.HBM))


def sizes(queries, pos):
    per_device, slots = pos.shape
    wide = (queries.shape[1] // DH) * BLOCK
    flops = 2 * slots * per_device * wide * BLOCK * DH
    return per_device, slots, (slots - 1) // 2, wide, flops


def forward(heads, slots, holder, queries, cotangent, gain, gathered):
    per_device, count, pairs, wide, flops = sizes(queries, slots)
    smem, vmem, hbm = specs()
    gathered = [pltpu.with_memory_space_constraint(g, pltpu.HBM) for g in gathered]
    return pl.pallas_call(
        lambda *refs: forward_kernel(pairs, 1.0 / math.sqrt(DH), math.log(BLOCK * count), *refs),
        out_shape=(
            jax.ShapeDtypeStruct((per_device, DH, wide), F32),
            jax.ShapeDtypeStruct((per_device, count * BLOCK, wide), F32),
            jax.ShapeDtypeStruct(((per_device * count + 1) * BLOCK, 2 * DH), BF16),
            jax.ShapeDtypeStruct((heads, 2 * per_device, BLOCK), F32),
        ),
        in_specs=[smem, smem, vmem, vmem, vmem] + [hbm] * len(GATHERED),
        out_specs=(vmem,) * 4,
        scratch_shapes=[pltpu.SemaphoreType.DMA((per_device * count,))],
        compiler_params=pltpu.CompilerParams(vmem_limit_bytes=8 << 20),
        cost_estimate=pl.CostEstimate(flops=2 * flops, bytes_accessed=16 << 20, transcendentals=0),
        name="forward",
    )(slots, holder, queries, cotangent, gain, *gathered)


def backward(heads, slots, holder, sums, queries, cotangent, gain, attended, weights, held):
    per_device, count, pairs, wide, flops = sizes(queries, slots)
    smem, vmem, _ = specs()
    columns = float(queries.shape[1] * heads)
    return pl.pallas_call(
        lambda *refs: backward_kernel(pairs, 1.0 / math.sqrt(DH), columns, *refs),
        out_shape=(jax.ShapeDtypeStruct((per_device, count * BLOCK, wide), BF16),)
        + tuple(jax.ShapeDtypeStruct((n * PART, 2 * DH), BF16) for n in SENT),
        in_specs=[smem, smem] + [vmem] * 7,
        out_specs=(vmem,) * (1 + len(SENT)),
        scratch_shapes=[pltpu.VMEM(((per_device * count + 1) * BLOCK, 2 * DH), F32)],
        compiler_params=pltpu.CompilerParams(vmem_limit_bytes=14 << 20),
        cost_estimate=pl.CostEstimate(flops=3 * flops, bytes_accessed=32 << 20, transcendentals=0),
        name="backward",
    )(slots, holder, sums, queries, cotangent, gain, attended, weights, held)


def finish(heads, slots, sums, gain, attended, scores, held):
    per_device, count, pairs, wide, _ = sizes(gain, slots)
    smem, vmem, _ = specs()
    width = gain.shape[1]
    grads = jax.ShapeDtypeStruct((per_device * BLOCK, width), BF16)
    flops = 2 * count * per_device * wide * BLOCK * DH
    return pl.pallas_call(
        lambda *refs: finish_kernel(pairs, 1.0 / math.sqrt(DH), float(width * heads), *refs),
        out_shape=(grads, grads),
        in_specs=[smem] + [vmem] * 5,
        out_specs=(vmem, vmem),
        compiler_params=pltpu.CompilerParams(vmem_limit_bytes=8 << 20),
        cost_estimate=pl.CostEstimate(flops=flops, bytes_accessed=8 << 20, transcendentals=0),
        name="finish",
    )(slots, sums, gain, attended, scores, held)


def body(queries, keys, values, cotangent, gain, key_blocks, span_order):
    key_width = keys.shape[1]
    heads = lax.axis_size(HEAD)
    gain = gain.reshape(1, queries.shape[1])
    gathered = gather_blocks(jnp.concatenate([keys, values], axis=1))
    slots, source_of, back_of = positions(key_blocks, span_order, queries.shape[0] // BLOCK)
    attended, weights, held, sums = forward(
        heads, slots, source_of, queries, cotangent, gain, gathered
    )
    sums = head_copies(sums)
    scores, *parts = backward(
        heads, slots, back_of, sums, queries, cotangent, gain, attended, weights, held
    )
    grads = scatter_blocks(*parts).astype(BF16)
    output, query_grad = finish(heads, slots, sums, gain, attended, scores, held)
    return output, query_grad, grads[:, :key_width], grads[:, key_width:]


def solution(mesh):
    fine = Mesh(mesh.devices.reshape(NZ, 2, 2, 4, 2), CTX + HEAD)
    tok = P(CTX, HEAD)
    return jax.shard_map(
        body,
        mesh=fine,
        in_specs=(tok, tok, tok, tok, P(HEAD), P(), P()),
        out_specs=(tok, tok, tok, tok),
        check_vma=False,
    )
```

```python
import math

import jax
import jax.numpy as jnp
from jax import lax
from jax.experimental import pallas as pl
from jax.experimental.pallas import tpu as pltpu
from jax.sharding import Mesh, PartitionSpec as P


DH = 128
BLOCK = 128
CTX = ("z", "xh", "core")
HEAD = ("y", "xl")
RING = ("z", "core")
NZ = 16
HALF = NZ // 2
SWAP = [(0, 1), (1, 0)]
NBLK = 128
PART = 4 * BLOCK
SWAP_AFTER = (2, 5, 7)
GATHERED = [1] * 16 + [4, 6, 4, 1, 1]
SENT = [16, 6, 4, 4, 1, 1]
F32 = jnp.float32
BF16 = jnp.bfloat16


def ring_pairs():
    return [
        (z * 2 + c, ((z + (1 if c == 0 else -1)) % NZ) * 2 + c) for z in range(NZ) for c in range(2)
    ]


def ring(x):
    return lax.ppermute(x, RING, ring_pairs())


def swap(x):
    return lax.ppermute(x, "core", SWAP)


def gather_blocks(kv):
    core = lax.axis_index("core")
    four = lax.all_gather(kv, ("xh", "core")).reshape(2, 2, *kv.shape)
    own, other = (
        lax.dynamic_index_in_dim(four, c, 1, keepdims=False).reshape(PART, kv.shape[1])
        for c in (core, 1 - core)
    )
    chunk, mine, theirs = [own, other], [], []
    waiting = []
    for s in range(1, HALF):
        own, other = ring(own), ring(other)
        mine += [own, other]
        waiting += [other, own]
        if s in SWAP_AFTER:
            theirs.append(swap(jnp.concatenate(waiting, axis=0)))
            waiting = []
    return chunk + mine + theirs + [ring(own), ring(other)]


def beside(a, b):
    none, width = (0, 0, 0), (0, a.shape[1], 0)
    zero = jnp.zeros((), a.dtype)
    return lax.pad(a, zero, (none, width)) + lax.pad(b, zero, (none, width[1::-1] + (0,)))


def total(*terms):
    out = terms[0].astype(F32)
    for t in terms[1:]:
        out = out + t.astype(F32)
    return out


def part_of(array, i):
    return array[i * PART : (i + 1) * PART]


def scatter_blocks(mine, near, middle, distant, *far):
    own, other = far
    near, middle, distant = swap(near), swap(middle), swap(distant)
    for s in range(HALF - 1, 0, -1):
        theirs, base = (distant, 6) if s > 5 else (middle, 4) if s > 3 else (near, 1)
        i = 2 * (s - base)
        other = ring(other)
        other = total(other, part_of(mine, 2 * s + 1), part_of(theirs, i)).astype(BF16)
        other, later_mine, later_theirs = lax.optimization_barrier((other, mine, theirs))
        own = ring(own)
        own = total(own, part_of(later_mine, 2 * s), part_of(later_theirs, i + 1)).astype(BF16)
    rows = PART // 2
    other = total(ring(other), part_of(mine, 1)).astype(BF16)
    other, mine = lax.optimization_barrier((other, mine))
    own = ring(own)
    own = total(own, part_of(mine, 0), swap(other))
    first = lax.axis_index("xh") == 0
    low, high = own[:rows], own[rows:]
    give = jnp.where(first, high, low).astype(BF16)
    pair = lax.all_gather(give, "xh")
    return total(jnp.where(first, low, high), jnp.where(first, pair[1], pair[0]))


def head_copies(x):
    return lax.all_to_all(x, HEAD, 0, 0, tiled=True)


def positions(key_blocks, span_order, per_device):
    z, xh, core = (lax.axis_index(n) for n in CTX)
    me = (z * 2 + xh) * 2 + core
    seq = lax.dynamic_slice(span_order, (me * per_device,), (per_device,))
    pick = (seq[:, None] == jnp.arange(NBLK)[None, :]).astype(jnp.int32)
    far = jnp.sum(pick[:, :, None] * key_blocks[None], axis=1)
    where = jnp.arange(NBLK, dtype=jnp.int32)
    store = jnp.sum(
        jnp.where(far[:, :, None] == span_order[None, None, :], where[None, None, :], 0), axis=2
    )
    own = me * per_device + jnp.arange(per_device, dtype=jnp.int32)
    store = jnp.concatenate([own[:, None], store], axis=1)
    live = jnp.concatenate([jnp.ones((per_device, 1), bool), far >= 0], axis=1)
    owner, half = store // per_device, store % per_device
    oz, oxh, ocore = owner // 4, (owner // 2) % 2, owner % 2
    dz = (oz - z + HALF) % NZ - HALF
    inner = oxh * 2 + half
    dist = jnp.abs(dz)

    across = ocore ^ core

    def locate(first_group):
        chunk = jnp.where(first_group, 0, 14) + 2 * dist
        chunk = jnp.where(dist == 0, 0, jnp.where(dist == HALF, 30, chunk))
        return jnp.where(live, (chunk + across) * 4 + inner, NBLK).reshape(-1)

    def holder(spot):
        match = spot[None, :] == jnp.arange(NBLK, dtype=jnp.int32)[:, None]
        return jnp.max(jnp.where(match, slot[None, :], -1), axis=1)

    source = locate((dz < 0) == (core == 0))
    count = source.shape[0]
    order = jnp.arange(count, dtype=jnp.int32)
    same = source[:, None] == source[None, :]
    first = jnp.min(jnp.where(same, order[None, :], count), axis=1)
    slot = jnp.where(source == NBLK, count, first).astype(jnp.int32)
    back = locate((dz > 0) == (core == 0))
    return slot.reshape(per_device, -1), holder(source), holder(back)


def rows_of(spot):
    return pl.ds(pl.multiple_of(spot * BLOCK, BLOCK), BLOCK)


def contract_first(a, b):
    return lax.dot_general(a, b, (((0,), (0,)), ((), ())), preferred_element_type=F32)


def dot(a, b):
    return jnp.dot(a, b, preferred_element_type=F32)


def heads_of(ref, q, n):
    return [ref[pl.ds(q * BLOCK, BLOCK), h * DH : (h + 1) * DH] for h in range(n)]


def each_block(counts, visit):
    base = 0
    for k, n in enumerate(counts):

        def one(i, carry, k=k, base=base):
            visit(k, i, base + i)
            return carry

        lax.fori_loop(0, 4 * n, one, 0, unroll=4)
        base += 4 * n


def steps_at(i):
    if isinstance(i, int) and i == 0:
        return 0, BLOCK
    return pl.multiple_of(BLOCK + 2 * BLOCK * (i - 1), BLOCK), 2 * BLOCK


def causal_mask(width):
    key = lax.broadcasted_iota(jnp.int32, (BLOCK, width), 0)
    row = lax.broadcasted_iota(jnp.int32, (BLOCK, width), 1) % BLOCK
    return key <= row


def forward_kernel(pairs, scale, shift, slots, holder, queries, cotangent, gain, *rest):
    n = len(GATHERED)
    sources, (attended, weights, held, sums, sems) = rest[:n], rest[n:]
    per_device = slots.shape[0]
    spare = per_device * slots.shape[1]
    group = queries.shape[1] // DH
    width = group * BLOCK

    def fetch(k, i, at):
        @pl.when(holder[at] >= 0)
        def _():
            pltpu.make_async_copy(
                sources[k].at[rows_of(i), :], held.at[rows_of(holder[at]), :], sems.at[holder[at]]
            ).start()

    def await_slot(q, j):
        mine = slots[q, j]

        @pl.when(mine == q * slots.shape[1] + j)
        def _():
            pltpu.make_async_copy(
                sources[0].at[:BLOCK, :], held.at[rows_of(mine), :], sems.at[mine]
            ).wait()

        return held[rows_of(mine), :]

    each_block(GATHERED, fetch)
    held[spare * BLOCK :, :] = jnp.zeros((BLOCK, 2 * DH), BF16)
    query_t = [
        jnp.concatenate([x.T for x in heads_of(queries, q, group)], axis=1)
        for q in range(per_device)
    ]

    def weigh(keys, query):
        score = dot(keys, query)
        return 1.0 / (1.0 + jnp.exp2(shift * math.log2(math.e) - score * (scale * math.log2(math.e))))

    for q in range(per_device):
        own = await_slot(q, 0)
        weight = jnp.where(causal_mask(width), weigh(own[:, :DH], query_t[q]), 0.0)
        weights[q, :BLOCK, :] = weight
        attended[q] = contract_first(own[:, DH:], weight.astype(BF16))

        def step(i, carry):
            two = jnp.concatenate([await_slot(q, 1 + 2 * i), await_slot(q, 2 + 2 * i)], axis=0)
            weight = weigh(two[:, :DH], query_t[q])
            weights[q, pl.ds(*steps_at(i + 1)), :] = weight
            attended[q] += contract_first(two[:, DH:], weight.astype(BF16))
            return carry

        lax.fori_loop(0, pairs, step, 0, unroll=True)
        att = attended[q]
        grad_in = jnp.concatenate(
            [
                (x.astype(F32) * gain[:, h * DH : (h + 1) * DH]).T
                for h, x in enumerate(heads_of(cotangent, q, group))
            ],
            axis=1,
        )
        for i, value in enumerate((att * att, grad_in * att)):
            col = jnp.sum(value, axis=0, keepdims=True)
            row = col[:, :BLOCK]
            for h in range(1, group):
                row = row + col[:, h * BLOCK : (h + 1) * BLOCK]
            sums[:, 2 * q + i : 2 * q + i + 1, :] = jnp.broadcast_to(
                row[None], (sums.shape[0], 1, BLOCK)
            )


def row_terms(q, columns, sums):
    squares = jnp.sum(sums[:, 2 * q, :], axis=0, keepdims=True)
    crossed = jnp.sum(sums[:, 2 * q + 1, :], axis=0, keepdims=True)
    return lax.rsqrt(squares / columns + 1e-6), crossed / columns


def backward_kernel(
    pairs, scale, columns, slots, holder, sums, queries, cotangent, gain, attended, weights, held, *rest
):
    scores, parts, acc = rest[0], rest[1:-1], rest[-1]
    per_device, count = slots.shape
    group = queries.shape[1] // DH
    for part in parts:
        part[...] = jnp.zeros(part.shape, BF16)
    grads_t, grads, stacked = [], [], []
    for q in range(per_device):
        inverse, inner = row_terms(q, columns, sums)
        back = inverse * inverse * inner
        grad_t, grad = [], []
        for h, x in enumerate(heads_of(cotangent, q, group)):
            gain_h = gain[:, h * DH : (h + 1) * DH]
            att = attended[q, :, h * BLOCK : (h + 1) * BLOCK]
            grad_in = (x.astype(F32) * gain_h).T
            low = inverse * (grad_in - att * back)
            grad_t.append(low.astype(BF16))
            grad.append(low.T.astype(BF16))
        grads_t.append(jnp.concatenate(grad_t, axis=1))
        grads.append(jnp.concatenate(grad, axis=0))
        stacked.append(jnp.concatenate(heads_of(queries, q, group), axis=0))

    def pair_grads(q, both, span):
        weight = weights[q, span, :]
        grad_weight = dot(both[:, DH:], grads_t[q])
        grad_score = (grad_weight * (weight * (1.0 - weight))).astype(BF16)
        scores[q, span, :] = grad_score
        low = weight.astype(BF16)
        return jnp.concatenate([dot(grad_score, stacked[q]) * scale, dot(low, grads[q])], axis=1)

    def keep_part(q, j, part):
        slot = slots[q, j]
        if q > 0:
            again = slot < q * count
            part = part + jnp.where(again, acc[rows_of(slot), :], 0.0)
        acc[rows_of(slot), :] = part

    for q in range(per_device):
        keep_part(q, 0, pair_grads(q, held[rows_of(slots[q, 0]), :], pl.ds(0, BLOCK)))

        def step(i, carry):
            part = pair_grads(q, pair_of(held, slots, q, i), pl.ds(*steps_at(i + 1)))
            keep_part(q, 1 + 2 * i, part[:BLOCK])
            keep_part(q, 2 + 2 * i, part[BLOCK:])
            return carry

        lax.fori_loop(0, pairs, step, 0, unroll=True)

    def hand_over(k, i, at):
        @pl.when(holder[at] >= 0)
        def _():
            parts[k][rows_of(i), :] = acc[rows_of(holder[at]), :].astype(BF16)

    each_block(SENT, hand_over)


def pair_of(held, slots, q, i):
    return jnp.concatenate(
        [held[rows_of(slots[q, 1 + 2 * i]), :], held[rows_of(slots[q, 2 + 2 * i]), :]], axis=0
    )


def finish_kernel(
    pairs, scale, columns, slots, sums, gain, attended, scores, held, output, query_grad
):
    per_device = slots.shape[0]
    group = output.shape[1] // DH
    for q in range(per_device):
        rows = pl.ds(q * BLOCK, BLOCK)
        inverse, _ = row_terms(q, columns, sums)
        for h in range(group):
            span = slice(h * DH, (h + 1) * DH)
            att = attended[q, :, h * BLOCK : (h + 1) * BLOCK]
            output[rows, span] = ((att * inverse).T * gain[:, span]).astype(BF16)
        grad = contract_first(held[rows_of(slots[q, 0]), :DH], scores[q, :BLOCK, :])

        def step(i, grad):
            two = pair_of(held, slots, q, i)[:, :DH]
            return grad + contract_first(two, scores[q, pl.ds(*steps_at(i + 1)), :])

        grad = lax.fori_loop(0, pairs, step, grad, unroll=True)
        for h in range(group):
            query_grad[rows, h * DH : (h + 1) * DH] = (
                grad[:, h * BLOCK : (h + 1) * BLOCK].T * scale
            ).astype(BF16)


def specs():
    return tuple(pl.BlockSpec(memory_space=m) for m in (pltpu.SMEM, pltpu.VMEM, pltpu.HBM))


def sizes(queries, pos):
    per_device, slots = pos.shape
    wide = (queries.shape[1] // DH) * BLOCK
    flops = 2 * slots * per_device * wide * BLOCK * DH
    return per_device, slots, (slots - 1) // 2, wide, flops


def forward(heads, slots, holder, queries, cotangent, gain, gathered):
    per_device, count, pairs, wide, flops = sizes(queries, slots)
    smem, vmem, hbm = specs()
    gathered = [pltpu.with_memory_space_constraint(g, pltpu.HBM) for g in gathered]
    return pl.pallas_call(
        lambda *refs: forward_kernel(pairs, 1.0 / math.sqrt(DH), math.log(BLOCK * count), *refs),
        out_shape=(
            jax.ShapeDtypeStruct((per_device, DH, wide), F32),
            jax.ShapeDtypeStruct((per_device, count * BLOCK, wide), F32),
            jax.ShapeDtypeStruct(((per_device * count + 1) * BLOCK, 2 * DH), BF16),
            jax.ShapeDtypeStruct((heads, 2 * per_device, BLOCK), F32),
        ),
        in_specs=[smem, smem, vmem, vmem, vmem] + [hbm] * len(GATHERED),
        out_specs=(vmem,) * 4,
        scratch_shapes=[pltpu.SemaphoreType.DMA((per_device * count,))],
        compiler_params=pltpu.CompilerParams(vmem_limit_bytes=8 << 20),
        cost_estimate=pl.CostEstimate(flops=2 * flops, bytes_accessed=16 << 20, transcendentals=0),
        name="forward",
    )(slots, holder, queries, cotangent, gain, *gathered)


def backward(heads, slots, holder, sums, queries, cotangent, gain, attended, weights, held):
    per_device, count, pairs, wide, flops = sizes(queries, slots)
    smem, vmem, _ = specs()
    columns = float(queries.shape[1] * heads)
    return pl.pallas_call(
        lambda *refs: backward_kernel(pairs, 1.0 / math.sqrt(DH), columns, *refs),
        out_shape=(jax.ShapeDtypeStruct((per_device, count * BLOCK, wide), BF16),)
        + tuple(jax.ShapeDtypeStruct((n * PART, 2 * DH), BF16) for n in SENT),
        in_specs=[smem, smem] + [vmem] * 7,
        out_specs=(vmem,) * (1 + len(SENT)),
        scratch_shapes=[pltpu.VMEM(((per_device * count + 1) * BLOCK, 2 * DH), F32)],
        compiler_params=pltpu.CompilerParams(vmem_limit_bytes=14 << 20),
        cost_estimate=pl.CostEstimate(flops=3 * flops, bytes_accessed=32 << 20, transcendentals=0),
        name="backward",
    )(slots, holder, sums, queries, cotangent, gain, attended, weights, held)


def finish(heads, slots, sums, gain, attended, scores, held):
    per_device, count, pairs, wide, _ = sizes(gain, slots)
    smem, vmem, _ = specs()
    width = gain.shape[1]
    grads = jax.ShapeDtypeStruct((per_device * BLOCK, width), BF16)
    flops = 2 * count * per_device * wide * BLOCK * DH
    return pl.pallas_call(
        lambda *refs: finish_kernel(pairs, 1.0 / math.sqrt(DH), float(width * heads), *refs),
        out_shape=(grads, grads),
        in_specs=[smem] + [vmem] * 5,
        out_specs=(vmem, vmem),
        compiler_params=pltpu.CompilerParams(vmem_limit_bytes=8 << 20),
        cost_estimate=pl.CostEstimate(flops=flops, bytes_accessed=8 << 20, transcendentals=0),
        name="finish",
    )(slots, sums, gain, attended, scores, held)


def body(queries, keys, values, cotangent, gain, key_blocks, span_order):
    key_width = keys.shape[1]
    heads = lax.axis_size(HEAD)
    gain = gain.reshape(1, queries.shape[1])
    gathered = gather_blocks(beside(keys, values))
    slots, source_of, back_of = positions(key_blocks, span_order, queries.shape[0] // BLOCK)
    attended, weights, held, sums = forward(
        heads, slots, source_of, queries, cotangent, gain, gathered
    )
    sums = head_copies(sums)
    scores, *parts = backward(
        heads, slots, back_of, sums, queries, cotangent, gain, attended, weights, held
    )
    grads = scatter_blocks(*parts).astype(BF16)
    output, query_grad = finish(heads, slots, sums, gain, attended, scores, held)
    return output, query_grad, grads[:, :key_width], grads[:, key_width:]


def solution(mesh):
    fine = Mesh(mesh.devices.reshape(NZ, 2, 2, 4, 2), CTX + HEAD)
    tok = P(CTX, HEAD)
    return jax.shard_map(
        body,
        mesh=fine,
        in_specs=(tok, tok, tok, tok, P(HEAD), P(), P()),
        out_specs=(tok, tok, tok, tok),
        check_vma=False,
    )
```
